32 devices in a mesh: frames: 8 (over z, y), rows: 4 (over x, core).
Axes of the slice: x: 2, y: 2, z: 4, core: 2. Of those that a mesh axis runs over, the one named last changes fastest.
Arguments:
- features: bfloat16 [8, 64, 128, 128], P('frames', 'rows'), may hold values from -6 to 6
- pair_weight: bfloat16 [8, 64, 4, 128, 128], P('frames', 'rows'), may hold values from -0.5 to 0.5
- target_tile: int32 [8, 64, 4], P('frames', 'rows'), may hold values from 0 to 31, all different within a row; in each aligned block of 16 rows (0 to 15, 16 to 31, ..., all dimensions but the last counted through in order) at most 4 rows name the same one
- target_block: int32 [8, 64, 4], P('frames', 'rows'), may hold values from 0 to 15
- conv1_weight: bfloat16 [3, 3, 3, 128, 128], replicated, may hold values from -0.109375 to 0.109375
- conv1_bias: float32 [128], replicated, may hold values from -3 to 3
- conv2_weight: bfloat16 [3, 3, 3, 128, 128], replicated, may hold values from -0.109375 to 0.109375
- conv2_bias: float32 [128], replicated, may hold values from -3 to 3
Outputs:
- occupancy: bfloat16 [64, 256, 4, 128], P('frames', 'rows')
The draws below stay inside these ranges and needn't reach their ends.
Inputs may be any that keep to these rules, and one draw needn't show every extreme that they name: `target_tile`: each image block names 4 different tiles; among the pairs of one device no tile is named more than 4 times, a bound that some block reaches.
All inputs are finite; a program needn't handle non-finite values.
Results may differ from the reference program's by a relative error of at most 0.0055.
Values may be sent and summed in bfloat16 or wider, within the bound.
No kernel may reach another device: no remote copies, remote signals or barrier semaphores. Data moves between devices by JAX's collectives and lax.ppermute only.
A program may use at most 128 MiB of HBM per device.

```python
import math
import jax
import jax.numpy as jnp
import numpy as np
from jax import lax

C = 128
VB = 128
TOP = 4
DEPTH = 4
IMG_DEV = 16
TX = 8
TY = 64
FRAMES = 8
BLOCKS = 64
VOXB = 16
CAP = 4
N_FRAMES = 8
N_ROWS = 4


def set_ends(drawn, stream_key, smallest, high):
    longest = drawn.shape.index(max(drawn.shape))
    spots = []
    for shift in (0, 1):
        where = [jax.random.randint(jax.random.fold_in(stream_key, axis), (), 0, length) for axis, length in enumerate(drawn.shape)]
        where[longest] = (where[longest] + shift) % drawn.shape[longest]
        spots.append(tuple(where))
    return drawn.at[spots[0]].set(smallest).at[spots[1]].set(high)


def block_levels(stream_key, shape, shards, least, high):
    loudness, own = 1.0, jax.random.fold_in(stream_key, 6)
    for axis_at, blocks in shards:
        steps = jnp.exp(jax.random.uniform(jax.random.fold_in(own, axis_at), (blocks,), jnp.float32, least / len(shards), high / len(shards)))
        loudness = loudness * jnp.repeat(steps, shape[axis_at] // blocks).reshape([-1 if axis == axis_at else 1 for axis in range(len(shape))])
    return loudness


def assign_block(rng, own, number, rows, amount, top, reach, slope):
    order = jax.random.permutation(rng, amount)
    packed, ordinary = load_shares(amount, rows * top, reach, slope, True), load_shares(amount, rows * top, reach, slope, False)
    places = jnp.arange(amount)

    def named(tallies, rotation):
        used = int((tallies > 0).sum())
        fixed = max(1, used // 4)
        passed = fixed + (places - fixed + rotation * (used - fixed)) % max(1, amount - fixed)
        return jnp.zeros((amount,), jnp.int32).at[order[jnp.where(places < fixed, places, passed)]].set(jnp.asarray(tallies, jnp.int32))

    tallies = jnp.where(number % 4 == 0, named(packed, number // 4), named(ordinary, number - number // 4 - 1))
    mixed = jax.random.permutation(jax.random.fold_in(own, 3), amount)
    source_of, receiver = mixed[0:amount // 2 * 2:2], mixed[1:amount // 2 * 2:2]
    slack = jnp.minimum(tallies[source_of] - 1, reach - tallies[receiver]) // 2
    slack = jnp.where((source_of == order[0]) | (receiver == order[0]) | (tallies[receiver] == 0), 0, jnp.maximum(slack, 0))
    passed = jax.random.randint(jax.random.fold_in(own, 4), (amount // 2,), 0, 1 << 20) % (slack + 1)
    tallies = tallies.at[source_of].add(-passed).at[receiver].add(passed)
    members = jnp.searchsorted(jnp.cumsum(tallies), jnp.arange(rows * top), side="right").astype(jnp.int32)
    listing = members.reshape(top, rows).T
    listing = listing[jax.random.permutation(jax.random.fold_in(own, 1), rows)]
    rotation = jax.random.randint(jax.random.fold_in(own, 2), (rows, 1), 0, top)
    return jnp.take_along_axis(listing, (jnp.arange(top)[None, :] + rotation) % top, axis=1)


def load_shares(amount, total, limit, slope, full):
    loads = [(1 << 20) // math.isqrt(grade ** slope) + 1 for grade in range(1, amount + 1)]
    largest = limit if full else min(limit, max(-(-total // amount), total * loads[0] // sum(loads)))
    least = 1 if total - largest >= amount - 1 else 0
    counts, spare = [largest] + [least] * (amount - 1), total - largest - least * (amount - 1)
    while spare > 0:
        free = [i for i in range(1, amount) if counts[i] < largest] or [i for i in range(1, amount) if counts[i] < limit]
        whole, budget = sum([loads[i] for i in free]), spare
        for i in free:
            addition = min(limit - counts[i], max(1, budget * loads[i] // whole), spare)
            counts[i] = counts[i] + addition
            spare = spare - addition
    return np.array(counts)


def bell_draw(key, extent, width, bound, pieces=(), kind=jnp.bfloat16):
    loudness = block_levels(key, extent, pieces, -0.22, 0.18) if pieces else 1.0
    array = jax.random.normal(key, extent, jnp.float32) * width * loudness
    return jnp.minimum(jnp.maximum(array, -bound), bound).astype(kind)


def setup_inputs(seed: int = 0) -> dict:
    keys = jax.random.split(jax.random.key(seed), 9)
    features = bell_draw(keys[0], (FRAMES, BLOCKS, VB, C), 1.0, 6.0, ((0, 8), (1, 4)))
    pair_weight = bell_draw(keys[1], (FRAMES, BLOCKS, TOP, VB, VB), VB ** -0.5, 0.5, ((0, 8), (1, 4)))
    target_tile_keys = jax.random.split(jax.random.fold_in(keys[2], 1), FRAMES * BLOCKS // IMG_DEV)
    target_tile_turns = jax.random.permutation(jax.random.fold_in(keys[2], 3), FRAMES * BLOCKS // IMG_DEV)
    target_tile = jax.vmap(lambda own, number: assign_block(jax.random.fold_in(keys[2], 2), own, number, IMG_DEV, N_FRAMES * N_ROWS, TOP, CAP, 2))(target_tile_keys, target_tile_turns).reshape((FRAMES, BLOCKS, TOP))
    target_block = set_ends(jax.random.randint(keys[3], (FRAMES, BLOCKS, TOP), 0, VOXB), jax.random.fold_in(keys[3], 1), 0, VOXB - 1).astype(jnp.int32)
    conv1_weight = bell_draw(keys[4], (3, 3, 3, C, C), (27 * C) ** -0.5, 0.109375)
    conv1_bias = bell_draw(keys[5], (C,), 0.5, 3.0, (), jnp.float32)
    conv2_weight = bell_draw(keys[6], (3, 3, 3, C, C), (27 * C) ** -0.5, 0.109375)
    conv2_bias = bell_draw(keys[7], (C,), 0.5, 3.0, (), jnp.float32)
    return dict(features=features, pair_weight=pair_weight, target_tile=target_tile, target_block=target_block, conv1_weight=conv1_weight, conv1_bias=conv1_bias, conv2_weight=conv2_weight, conv2_bias=conv2_bias)


def convolve(volume, weight, bias):
    summed = lax.conv_general_dilated(volume.astype(jnp.float32), weight.astype(jnp.float32), (1, 1, 1), "SAME", dimension_numbers=("NDHWC", "DHWIO", "NDHWC"), preferred_element_type=jnp.float32)
    return jax.nn.silu(summed + bias).astype(jnp.bfloat16)


def reference(features, pair_weight, target_tile, target_block, conv1_weight, conv1_bias, conv2_weight, conv2_bias):
    tiles = N_FRAMES * N_ROWS

    def add_frame(volume, items):
        frame_feat, frame_weight, frame_tile, frame_block = items
        contribution = jnp.einsum("btvp,bpc->btvc", frame_weight.astype(jnp.float32), frame_feat.astype(jnp.float32))
        block_ids = (frame_tile * VOXB + frame_block).reshape(-1).astype(jnp.int32)
        return volume.at[block_ids].add(contribution.reshape(-1, VB, C)), None

    start = jnp.zeros((tiles * VOXB, VB, C), jnp.float32)
    blocks, _ = lax.scan(add_frame, start, (features, pair_weight, target_tile, target_block))
    grid = blocks.astype(jnp.bfloat16).reshape(N_FRAMES, N_ROWS, TX, TY, DEPTH, C)
    grid = grid.transpose(0, 2, 1, 3, 4, 5).reshape(1, TX * N_FRAMES, TY * N_ROWS, DEPTH, C)
    hidden = convolve(grid, conv1_weight, conv1_bias)
    occupancy = convolve(hidden, conv2_weight, conv2_bias)
    return occupancy[0]
```

```python
import functools

import jax
import jax.numpy as jnp
from jax import lax
from jax.experimental import pallas as pl
from jax.experimental.pallas import tpu as pltpu
from jax.sharding import PartitionSpec as P

DEPTH = 4
TX = 8
TY = 64
LABEL_ROWS = 16
VMEM = pltpu.VMEM
LIMIT = 60 * 1024 * 1024


def vmem():
    return pl.BlockSpec(memory_space=pltpu.VMEM)


def smem():
    return pl.BlockSpec(memory_space=pltpu.SMEM)


def contribute_kernel(tiles, capacity, top, tile_ref, block_ref, weight_ref, feature_ref, out_ref, counts, labels):
    images = feature_ref.shape[0]
    size = feature_ref.shape[1]

    def clear(t, carry):
        counts[t] = 0
        for k in range(capacity):
            labels[t * capacity + k] = -1
        return carry

    lax.fori_loop(0, tiles, clear, 0)

    def image(b, carry):
        weights = weight_ref[b].reshape(top * size, size)
        product = jnp.dot(weights, feature_ref[b], preferred_element_type=jnp.float32)
        product = product.astype(jnp.bfloat16)
        for t in range(top):
            tile = tile_ref[b * top + t]
            rank = counts[tile]
            counts[tile] = rank + 1
            labels[tile * capacity + rank] = block_ref[b * top + t]
            out_ref[tile, pl.ds(pl.multiple_of(rank * size, size), size), :] = product[t * size : (t + 1) * size]
        return carry

    lax.fori_loop(0, images, image, 0)
    lane = lax.broadcasted_iota(jnp.int32, (LABEL_ROWS, out_ref.shape[2]), 1)

    def mark(t, carry):
        row = jnp.full(lane.shape, -1, jnp.int32)
        for k in range(capacity):
            row = jnp.where(lane == k, labels[t * capacity + k], row)
        out_ref[t, capacity * size :, :] = row.astype(jnp.float32).astype(jnp.bfloat16)
        return carry

    lax.fori_loop(0, tiles, mark, 0)


def gather_kernel(tiles, capacity, size, received_ref, out_ref, total, marks, marks_smem, sem):
    base = capacity * size

    def read(t, carry):
        row = received_ref[t, base : base + LABEL_ROWS, :].astype(jnp.float32)
        marks[pl.ds(t, 1), :] = row[0:1, :].astype(jnp.int32)
        return carry

    lax.fori_loop(0, tiles, read, 0)
    copy = pltpu.make_async_copy(marks, marks_smem, sem)
    copy.start()
    total[...] = jnp.zeros_like(total)
    copy.wait()

    def add(t, carry):
        for k in range(capacity):
            label = marks_smem[t, k]

            @pl.when(label >= 0)
            def _():
                rows = pl.ds(pl.multiple_of(label * size, size), size)
                total[rows, :] += received_ref[t, k * size : (k + 1) * size, :].astype(jnp.float32)

        return carry

    lax.fori_loop(0, tiles, add, 0)
    cells = total.shape[0] // DEPTH
    channels = total.shape[1]
    for z in range(DEPTH):
        part = total[pl.ds(z, cells, stride=DEPTH), :]
        out_ref[:, z * channels : (z + 1) * channels] = part.astype(jnp.bfloat16)


def band_kernel(first_ref, second_ref, out1_ref, out2_ref):
    channels = first_ref.shape[-1]
    zero = jnp.zeros((channels, channels), jnp.bfloat16)
    for source, target in ((first_ref, out1_ref), (second_ref, out2_ref)):
        for dx in range(3):
            for half in range(2):
                for dy in range(3):
                    for k in range(3):
                        z_in = k + half
                        for j in range(2):
                            dz = z_in - (2 * half + j) + 1
                            value = source[dx, dy, dz] if 0 <= dz < 3 else zero
                            row = (dy * 3 + k) * channels
                            target[dx, half, row : row + channels, j * channels : (j + 1) * channels] = value


def convolve_half(copies, bands, half, out_rows, channels):
    total = None
    for dx in range(3):
        pieces = []
        for dy in range(3):
            piece = copies[dy][dx : dx + out_rows, :, half * channels : (half + 3) * channels]
            pieces.append(piece.reshape(-1, 3 * channels))
        product = jnp.dot(
            jnp.concatenate(pieces, axis=1), bands[dx, half], preferred_element_type=jnp.float32
        )
        total = product if total is None else total + product
    return total


def silu(v):
    return v / (1.0 + jnp.exp(-v))


def convolve_kernel(
    ends_ref, main_ref, low_ref, high_ref, left_ref, right_ref,
    band1_ref, band2_ref, bias1_ref, bias2_ref, out_ref,
    copies0, copies1, copies2, hidden, shift1, shift2, stage,
):
    channels = bias1_ref.shape[1]
    rows, cols = main_ref.shape[0], main_ref.shape[1]
    for x0, source in ((0, low_ref), (2, main_ref), (2 + rows, high_ref)):
        value = source[...]
        part = slice(x0, x0 + value.shape[0])
        copies0[part, 2 : 2 + cols, :] = value
        copies1[part, 1 : 1 + cols, :] = value
        copies2[part, 0:cols, :] = value
    left = left_ref[...]
    right = right_ref[...]
    copies0[:, 0:2, :] = left
    copies1[:, 0:1, :] = left[:, 1:2]
    copies1[:, 1 + cols : 2 + cols, :] = right[:, 0:1]
    copies2[:, cols : 2 + cols, :] = right
    for half in range(2):
        total = convolve_half((copies0, copies1, copies2), band1_ref, half, rows + 2, channels)
        bias = jnp.concatenate([bias1_ref[...], bias1_ref[...]], axis=1)
        value = silu(total + bias).reshape(rows + 2, -1, 2 * channels)
        x_at = lax.broadcasted_iota(jnp.int32, value.shape, 0)
        y_at = lax.broadcasted_iota(jnp.int32, value.shape, 1)
        keep = (x_at >= ends_ref[0]) & (x_at < rows + 2 - ends_ref[1])
        keep = keep & (y_at >= ends_ref[2]) & (y_at < cols + 2 - ends_ref[3])
        value = jnp.where(keep, value, 0.0).astype(jnp.bfloat16)
        hidden[:, :, half * 2 * channels : (half + 1) * 2 * channels] = value
    shift1[...] = hidden[:, 1 : 1 + cols, :]
    shift2[...] = hidden[:, 2 : 2 + cols, :]
    for half in range(2):
        total = convolve_half(
            (hidden.at[:, 0:cols, :], shift1, shift2), band2_ref, half, rows, channels
        )
        for j in range(2):
            value = silu(total[:, j * channels : (j + 1) * channels] + bias2_ref[...])
            stage[pl.ds(2 * half + j, rows * cols, stride=DEPTH), :] = value
    out_ref[...] = stage[...].astype(jnp.bfloat16)


def shards(features, pair_weight, target_tile, target_block, conv1_weight, conv1_bias, conv2_weight, conv2_bias):
    images, size, channels = features.shape[1:]
    top = target_tile.shape[2]
    n_frames = lax.axis_size("frames")
    n_rows = lax.axis_size("rows")
    devices = n_frames * n_rows
    capacity = max(2, 2 * images * top // devices)
    message = capacity * size + LABEL_ROWS
    params = pltpu.CompilerParams(vmem_limit_bytes=LIMIT)
    outgoing = pl.pallas_call(
        functools.partial(contribute_kernel, devices, capacity, top),
        out_shape=jax.ShapeDtypeStruct((devices, message, channels), jnp.bfloat16),
        in_specs=[smem(), smem(), vmem(), vmem()],
        out_specs=vmem(),
        scratch_shapes=[pltpu.SMEM((devices,), jnp.int32), pltpu.SMEM((devices * capacity,), jnp.int32)],
        compiler_params=params,
        name="contribute",
    )(target_tile.reshape(-1), target_block.reshape(-1), pair_weight[0], features[0])
    received = lax.all_to_all(outgoing, ("frames", "rows"), split_axis=0, concat_axis=0, tiled=True)
    cells = TX * TY
    grid = pl.pallas_call(
        functools.partial(gather_kernel, devices, capacity, size),
        out_shape=jax.ShapeDtypeStruct((cells, DEPTH * channels), jnp.bfloat16),
        in_specs=[vmem()],
        out_specs=vmem(),
        scratch_shapes=[
            VMEM((cells * DEPTH, channels), jnp.float32),
            VMEM((devices, channels), jnp.int32),
            pltpu.SMEM((devices, channels), jnp.int32),
            pltpu.SemaphoreType.DMA,
        ],
        compiler_params=params,
        name="gather",
    )(received)
    bands = jax.ShapeDtypeStruct((3, 2, 9 * channels, 2 * channels), jnp.bfloat16)
    band1, band2 = pl.pallas_call(
        band_kernel,
        out_shape=(bands, bands),
        in_specs=[vmem(), vmem()],
        out_specs=(vmem(), vmem()),
        compiler_params=params,
        name="bands",
    )(conv1_weight, conv2_weight)
    main = grid.reshape(TX, TY, DEPTH * channels)

    def shifted(value, axis, count, step):
        pairs = [(i, i + step) for i in range(count) if 0 <= i + step < count]
        return lax.ppermute(value, axis, pairs)

    low = shifted(main[TX - 2 :], "frames", n_frames, 1)
    high = shifted(main[:2], "frames", n_frames, -1)
    edge = jnp.concatenate([low[:, TY - 2 :], main[:, TY - 2 :], high[:, TY - 2 :]], axis=0)
    left = shifted(edge, "rows", n_rows, 1)
    edge = jnp.concatenate([low[:, :2], main[:, :2], high[:, :2]], axis=0)
    right = shifted(edge, "rows", n_rows, -1)
    f, r = lax.axis_index("frames"), lax.axis_index("rows")
    ends = jnp.stack([f == 0, f == n_frames - 1, r == 0, r == n_rows - 1]).astype(jnp.int32)
    wide = 80
    lanes = DEPTH * channels
    out = pl.pallas_call(
        convolve_kernel,
        out_shape=jax.ShapeDtypeStruct((cells * DEPTH, channels), jnp.bfloat16),
        in_specs=[smem()] + [vmem()] * 9,
        out_specs=vmem(),
        scratch_shapes=[VMEM((TX + 4, wide, lanes), jnp.bfloat16)] * 3
        + [VMEM((TX + 2, wide, lanes), jnp.bfloat16)]
        + [VMEM((TX + 2, TY, lanes), jnp.bfloat16)] * 2
        + [VMEM((cells * DEPTH, channels), jnp.float32)],
        compiler_params=params,
        name="convolve",
    )(ends, main, low, high, left, right, band1, band2, conv1_bias[None], conv2_bias[None])
    return out.reshape(TX, TY, DEPTH, channels)


def solution(mesh):
    placed = (
        P("frames", "rows", None, None),
        P("frames", "rows", None, None, None),
        P("frames", "rows", None),
        P("frames", "rows", None),
        P(),
        P(),
        P(),
        P(),
    )
    return jax.shard_map(
        shards,
        mesh=mesh,
        in_specs=placed,
        out_specs=P("frames", "rows", None, None),
        check_vma=False,
    )
```

```python
import functools

import jax
import jax.numpy as jnp
from jax import lax
from jax.experimental import pallas as pl
from jax.experimental.pallas import tpu as pltpu
from jax.sharding import PartitionSpec as P

DEPTH = 4
TX = 8
TY = 64
CORES = 2
PAIRS = 4
LABEL_ROWS = 16
VMEM = pltpu.VMEM
LIMIT = 60 * 1024 * 1024


def vmem():
    return pl.BlockSpec(memory_space=pltpu.VMEM)


def smem():
    return pl.BlockSpec(memory_space=pltpu.SMEM)


def anywhere():
    return pl.BlockSpec(memory_space=pl.ANY)


def params():
    return pltpu.CompilerParams(vmem_limit_bytes=LIMIT)


def arrays(count, rows, channels, dtype=jnp.bfloat16):
    return [jax.ShapeDtypeStruct((rows, channels), dtype)] * count


def split_low(value, count):
    if count & (count - 1) == 0:
        return value >> (count.bit_length() - 1), value & (count - 1)
    return value // count, value % count


def contribute_kernel(shape, capacity, top, chunk, first, *refs):
    n_z, n_y, n_x, n_c = shape
    groups = (n_x * n_c, n_y * n_c)
    locals_ = (n_z * n_y, n_z * n_x)
    if first:
        at_ref, tile_ref, block_ref, weight_ref, feature_ref = refs[:5]
        outs = refs[5 : 5 + sum(groups)]
        index_ref = refs[5 + sum(groups)]
        buffers = refs[6 + sum(groups) : 8 + sum(groups)]
        sems, counts, labels = refs[8 + sum(groups) :]
    else:
        index_in, weight_ref, feature_ref = refs[:3]
        refs = refs[3:]
        refs = refs[1:]
        outs = refs[: sum(groups)]
        buffers = refs[sum(groups) : sum(groups) + 2]
        (sems,) = refs[sum(groups) + 2 :]
        index_ref = index_in
    images = feature_ref.shape[0]
    pairs = images * top
    tiles = n_z * n_y * n_x * n_c
    if first:

        def clear(t, carry):
            counts[t] = 0
            for k in range(capacity):
                labels[t * capacity + k] = -1
                labels[(tiles + t) * capacity + k] = -1
            return carry

        lax.fori_loop(0, tiles, clear, 0)
        z, y, x, c = (at_ref[i] for i in range(4))

        def place(p, carry):
            tile = tile_ref[p]
            rank = counts[tile]
            counts[tile] = rank + 1
            rest, c_to = split_low(tile, n_c)
            rest, x_to = split_low(rest, n_x)
            z_to, y_to = split_low(rest, n_y)
            dz = split_low(z_to - z + n_z, n_z)[1]
            dy = split_low(y_to - y + n_y, n_y)[1]
            dx = split_low(x_to - x + n_x, n_x)[1]
            group = split_low((x_to * n_c + c_to) - (x * n_c + c) + n_x * n_c, n_x * n_c)[1]
            slot = ((group * n_y + dy) * n_z + dz) * capacity + rank
            index_ref[p] = slot
            labels[slot] = block_ref[p]
            group = split_low((y_to * n_c + c_to) - (y * n_c + c) + n_y * n_c, n_y * n_c)[1]
            slot = ((group * n_x + dx) * n_z + dz) * capacity + rank
            index_ref[pairs + p] = slot
            labels[tiles * capacity + slot] = block_ref[p]
            return carry

        lax.fori_loop(0, pairs, place, 0)

    def image(b, carry):
        weights = weight_ref[pl.ds(b * top, top)]
        weights = weights.reshape(top * 2 * chunk, weights.shape[2])
        product = jnp.dot(weights, feature_ref[b], preferred_element_type=jnp.float32)
        product = product.astype(jnp.bfloat16)
        for t in range(top):
            p = b * top + t
            for order in range(2):
                row = (2 * t + order) * chunk
                group, slot = split_low(index_ref[order * pairs + p], locals_[order] * capacity)
                buffers[order][group, pl.ds(pl.multiple_of(slot * chunk, chunk), chunk), :] = product[
                    row : row + chunk
                ]
        return carry

    lax.fori_loop(0, images, image, 0)
    if first:
        lane = lax.broadcasted_iota(jnp.int32, (LABEL_ROWS, feature_ref.shape[2]), 1)
        for order in range(2):
            slots = locals_[order] * capacity

            def mark(g, carry):
                row = jnp.full(lane.shape, -1, jnp.int32)
                for k in range(slots):
                    row = jnp.where(lane == k, labels[order * tiles * capacity + g * slots + k], row)
                buffers[order][g, slots * chunk :, :] = row.astype(jnp.float32).astype(jnp.bfloat16)
                return carry

            lax.fori_loop(0, groups[order], mark, 0)
    copies = []
    for order in range(2):
        for g in range(groups[order]):
            i = order * groups[0] + g
            copies.append(pltpu.make_async_copy(buffers[order].at[g], outs[i], sems.at[i]))
    for copy in copies:
        copy.start()
    for copy in copies:
        copy.wait()


def merge_kernel(shape, capacity, chunk, blocks, first, *refs):
    n_z, n_y, n_x, n_c = shape
    groups = (n_x * n_c, n_y * n_c)
    steps = (n_y, n_x)
    locals_ = (n_z * n_y, n_z * n_x)
    total_groups = sum(groups)
    messages = refs[:total_groups]
    refs = refs[total_groups:]
    if first:
        outs = refs[: sum(steps)]
        plan_ref, total, marks, marks_smem, sem = refs[sum(steps) :]
        for order in range(2):
            slots = locals_[order] * capacity
            for g in range(groups[order]):
                i = order * groups[0] + g
                row = messages[i][slots * chunk :, :].astype(jnp.float32)
                marks[i : i + 1, :] = row[0:1, :].astype(jnp.int32)
        copy = pltpu.make_async_copy(marks, marks_smem, sem)
        copy.start()
    else:
        plan_ref = refs[0]
        outs = refs[1 : 1 + sum(steps)]
        (total,) = refs[1 + sum(steps) :]
    total[...] = jnp.zeros_like(total)
    stride = max(locals_) * capacity + 1
    if first:
        copy.wait()
        for order in range(2):
            slots = locals_[order] * capacity
            for g in range(groups[order]):
                i = order * groups[0] + g

                def note(s, count):
                    label = marks_smem[i, s]
                    plan_ref[i * stride + 1 + count] = s * blocks + jnp.maximum(label, 0)
                    return count + (label >= 0).astype(jnp.int32)

                plan_ref[i * stride] = lax.fori_loop(0, slots, note, 0, unroll=4)
    base = 0
    for order in range(2):
        for g in range(groups[order]):
            i = order * groups[0] + g

            def add(n, carry):
                slot, label = split_low(plan_ref[i * stride + 1 + n], blocks)
                local = split_low(slot, capacity)[0]
                source = pl.ds(pl.multiple_of(slot * chunk, chunk), chunk)
                target = pl.ds(pl.multiple_of((base + local * blocks + label) * chunk, chunk), chunk)
                total[target, :] += messages[i][source, :].astype(jnp.float32)
                return carry

            lax.fori_loop(0, plan_ref[i * stride], add, 0)
        base += locals_[order] * blocks
    rows = n_z * blocks * chunk
    at = 0
    for out in outs:
        out[...] = total[at : at + rows, :].astype(jnp.bfloat16)
        at += rows


def combine_kernel(shape, chunk, blocks, *refs):
    n_z, n_y, n_x, _ = shape
    ins = (refs[:n_y], refs[n_y : n_y + n_x])
    outs = refs[n_y + n_x :]
    rows = blocks * chunk
    for dz in range(n_z):
        for order in range(2):
            value = None
            for ref in ins[order]:
                part = ref[dz * rows : (dz + 1) * rows, :].astype(jnp.float32)
                value = part if value is None else value + part
            outs[dz][order * rows : (order + 1) * rows, :] = value.astype(jnp.bfloat16)


def finish_kernel(n_z, chunk, blocks, *refs):
    parts = refs[: n_z * PAIRS]
    out_ref, low_ref, high_ref, total = refs[n_z * PAIRS :]
    size = 2 * PAIRS * chunk
    for k in range(PAIRS):
        for order in range(2):
            for block in range(blocks):
                row = (order * blocks + block) * chunk
                value = None
                for ref in parts[k * n_z : (k + 1) * n_z]:
                    part = ref[row : row + chunk, :].astype(jnp.float32)
                    value = part if value is None else value + part
                at = block * size + (2 * k + order) * chunk
                total[at : at + chunk, :] = value
    cells = total.shape[0] // DEPTH
    channels = total.shape[1]
    for z in range(DEPTH):
        part = total[pl.ds(z, cells, stride=DEPTH), :].astype(jnp.bfloat16)
        lanes = slice(z * channels, (z + 1) * channels)
        out_ref[:, lanes] = part
        low_ref[:, lanes] = part[: 2 * TY]
        high_ref[:, lanes] = part[cells - 2 * TY :]


def band_kernel(first_ref, second_ref, out1_ref, out2_ref):
    channels = first_ref.shape[-1]
    zero = jnp.zeros((channels, channels), jnp.bfloat16)
    for source, target in ((first_ref, out1_ref), (second_ref, out2_ref)):
        for dx in range(3):
            for half in range(2):
                for dy in range(3):
                    for k in range(3):
                        z_in = k + half
                        for j in range(2):
                            dz = z_in - (2 * half + j) + 1
                            value = source[dx, dy, dz] if 0 <= dz < 3 else zero
                            row = (dy * 3 + k) * channels
                            target[dx, half, row : row + channels, j * channels : (j + 1) * channels] = value


def convolve_half(copies, bands, half, out_rows, channels):
    total = None
    for dx in range(3):
        pieces = []
        for dy in range(3):
            piece = copies[dy][dx : dx + out_rows, :, half * channels : (half + 3) * channels]
            pieces.append(piece.reshape(-1, 3 * channels))
        product = jnp.dot(
            jnp.concatenate(pieces, axis=1), bands[dx, half], preferred_element_type=jnp.float32
        )
        total = product if total is None else total + product
    return total


def silu(v):
    return v / (1.0 + jnp.exp(-v))


def convolve_kernel(
    ends_ref, main_ref, low_ref, high_ref, left_ref, right_ref,
    band1_ref, band2_ref, bias1_ref, bias2_ref, out_ref,
    copies0, copies1, copies2, hidden, shift1, shift2, stage,
):
    channels = bias1_ref.shape[1]
    rows, cols = main_ref.shape[0], main_ref.shape[1]
    for x0, source in ((0, low_ref), (2, main_ref), (2 + rows, high_ref)):
        value = source[...]
        part = slice(x0, x0 + value.shape[0])
        copies0[part, 2 : 2 + cols, :] = value
        copies1[part, 1 : 1 + cols, :] = value
        copies2[part, 0:cols, :] = value
    left = left_ref[...]
    right = right_ref[...]
    copies0[:, 0:2, :] = left
    copies1[:, 0:1, :] = left[:, 1:2]
    copies1[:, 1 + cols : 2 + cols, :] = right[:, 0:1]
    copies2[:, cols : 2 + cols, :] = right
    for half in range(2):
        total = convolve_half((copies0, copies1, copies2), band1_ref, half, rows + 2, channels)
        bias = jnp.concatenate([bias1_ref[...], bias1_ref[...]], axis=1)
        value = silu(total + bias).reshape(rows + 2, -1, 2 * channels)
        x_at = lax.broadcasted_iota(jnp.int32, value.shape, 0)
        y_at = lax.broadcasted_iota(jnp.int32, value.shape, 1)
        keep = (x_at >= ends_ref[0]) & (x_at < rows + 2 - ends_ref[1])
        keep = keep & (y_at >= ends_ref[2]) & (y_at < cols + 2 - ends_ref[3])
        value = jnp.where(keep, value, 0.0).astype(jnp.bfloat16)
        hidden[:, :, half * 2 * channels : (half + 1) * 2 * channels] = value
    shift1[...] = hidden[:, 1 : 1 + cols, :]
    shift2[...] = hidden[:, 2 : 2 + cols, :]
    for half in range(2):
        total = convolve_half(
            (hidden.at[:, 0:cols, :], shift1, shift2), band2_ref, half, rows, channels
        )
        for j in range(2):
            value = silu(total[:, j * channels : (j + 1) * channels] + bias2_ref[...])
            stage[pl.ds(2 * half + j, rows * cols, stride=DEPTH), :] = value
    out_ref[...] = stage[...].astype(jnp.bfloat16)


def shards(features, pair_weight, target_tile, target_block, conv1_weight, conv1_bias, conv2_weight, conv2_bias):
    images, size, channels = features.shape[1:]
    top = target_tile.shape[2]
    n_frames = lax.axis_size("frames")
    n_rows = lax.axis_size("rows")
    devices = n_frames * n_rows
    capacity = max(2, 2 * images * top // devices)
    blocks = TX * TY * DEPTH // size
    n_c = CORES if n_rows % CORES == 0 else 1
    n_x = n_rows // n_c
    n_y = n_x if n_frames % n_x == 0 else 1
    n_z = n_frames // n_y
    shape = (n_z, n_y, n_x, n_c)
    chunk = size // (2 * PAIRS)
    groups = (n_x * n_c, n_y * n_c)
    locals_ = (n_z * n_y, n_z * n_x)
    steps = (n_y, n_x)

    def shifted(value, dz=0, dy=0, dx=0, dc=0, row=0, col=0):
        pairs = []
        for source in range(devices):
            f, r = divmod(source, n_rows)
            z, y = divmod(f, n_y)
            x, c = divmod(r, n_c)
            z, y, x = (z + dz) % n_z, (y + dy) % n_y, (x + dx) % n_x
            if row:
                x, c = divmod((x * n_c + c + row) % (n_x * n_c), n_c)
            if col:
                y, c = divmod((y * n_c + c + col) % (n_y * n_c), n_c)
            pairs.append((source, ((z * n_y + y) * n_x + x) * n_c + c))
        return lax.ppermute(value, ("frames", "rows"), pairs)

    f, r = lax.axis_index("frames"), lax.axis_index("rows")
    at = jnp.stack([f // n_y, f % n_y, r // n_c, r % n_c]).astype(jnp.int32)
    weights = pair_weight[0].reshape(images * top, size, size)
    tile_ids, block_ids = target_tile.reshape(-1), target_block.reshape(-1)
    index = None
    plan = None
    sums = []
    final = []
    stride = max(locals_) * capacity + 1

    def contribute(k, index, after):
        first = k == 0
        extra = LABEL_ROWS if first else 0
        rows = [locals_[o] * capacity * chunk + extra for o in range(2)]
        outs = arrays(groups[0], rows[0], channels) + arrays(groups[1], rows[1], channels)
        out_specs = [anywhere()] * len(outs)
        scratch = [VMEM((groups[o], rows[o], channels), jnp.bfloat16) for o in range(2)]
        scratch.append(pltpu.SemaphoreType.DMA((sum(groups),)))
        weight_spec = pl.BlockSpec((images * top, 2 * chunk, size), lambda i: (0, k, 0))
        feature_spec = pl.BlockSpec((images, size, channels), lambda i: (0, 0, 0))
        if first:
            outs.append(jax.ShapeDtypeStruct((2 * images * top,), jnp.int32))
            out_specs.append(smem())
            scratch.append(pltpu.SMEM((devices,), jnp.int32))
            scratch.append(pltpu.SMEM((2 * devices * capacity,), jnp.int32))
            in_specs = [smem(), smem(), smem(), weight_spec, feature_spec]
            args = (at, tile_ids, block_ids, weights, features[0])
        else:
            in_specs = [smem(), weight_spec, feature_spec, anywhere()]
            args = (index, weights, features[0], after)
        return pl.pallas_call(
            functools.partial(contribute_kernel, shape, capacity, top, chunk, first),
            grid=(1,),
            out_shape=tuple(outs),
            in_specs=in_specs,
            out_specs=tuple(out_specs),
            scratch_shapes=scratch,
            compiler_params=params(),
            name=f"contribute{k}",
        )(*args)

    def exchange(messages):
        received = []
        for i, value in enumerate(messages):
            if i < groups[0]:
                received.append(shifted(value, row=i) if i else value)
            else:
                g = i - groups[0]
                received.append(shifted(value, col=g) if g else value)
        return received

    def merge(k, messages, plan):
        first = k == 0
        rows = n_z * blocks * chunk
        outs = arrays(sum(steps), rows, channels)
        out_specs = [vmem()] * len(outs)
        scratch = [VMEM((rows * sum(steps), channels), jnp.float32)]
        in_specs = [vmem()] * len(messages)
        args = tuple(messages)
        if first:
            outs.append(jax.ShapeDtypeStruct((stride * sum(groups),), jnp.int32))
            out_specs.append(smem())
            scratch += [
                VMEM((sum(groups), channels), jnp.int32),
                pltpu.SMEM((sum(groups), channels), jnp.int32),
                pltpu.SemaphoreType.DMA,
            ]
        else:
            in_specs.append(smem())
            args += (plan,)
        return pl.pallas_call(
            functools.partial(merge_kernel, shape, capacity, chunk, blocks, first),
            out_shape=tuple(outs),
            in_specs=in_specs,
            out_specs=tuple(out_specs),
            scratch_shapes=scratch,
            compiler_params=params(),
            name=f"merge{k}",
        )(*args)

    def second(partials):
        received = []
        for i, value in enumerate(partials):
            if i < n_y:
                received.append(shifted(value, dy=i) if i else value)
            else:
                received.append(shifted(value, dx=i - n_y) if i > n_y else value)
        return received

    def combine(k, partials):
        return pl.pallas_call(
            functools.partial(combine_kernel, shape, chunk, blocks),
            out_shape=tuple(arrays(n_z, 2 * blocks * chunk, channels)),
            in_specs=[vmem()] * len(partials),
            out_specs=tuple([vmem()] * n_z),
            compiler_params=params(),
            name=f"combine{k}",
        )(*partials)

    lead = 2
    stage1, stage2 = {}, {}
    for k in range(min(lead, PAIRS)):
        made = contribute(k, index, None if k == 0 else index)
        if k == 0:
            index = made[-1]
            made = made[:-1]
        stage1[k] = exchange(made)
    for k in range(PAIRS):
        merged = merge(k, stage1[k], plan)
        if k == 0:
            plan = merged[-1]
            merged = merged[:-1]
        stage2[k] = second(merged)
        if k + lead < PAIRS:
            stage1[k + lead] = exchange(contribute(k + lead, index, merged[0]))
        parts = combine(k, stage2[k])
        final += [shifted(part, dz=dz) if dz else part for dz, part in enumerate(parts)]
    cells = TX * TY
    lanes = DEPTH * channels
    main, first_rows, last_rows = pl.pallas_call(
        functools.partial(finish_kernel, n_z, chunk, blocks),
        out_shape=(
            jax.ShapeDtypeStruct((cells, lanes), jnp.bfloat16),
            jax.ShapeDtypeStruct((2 * TY, lanes), jnp.bfloat16),
            jax.ShapeDtypeStruct((2 * TY, lanes), jnp.bfloat16),
        ),
        in_specs=[vmem()] * len(final),
        out_specs=(vmem(),) * 3,
        scratch_shapes=[VMEM((cells * DEPTH, channels), jnp.float32)],
        compiler_params=params(),
        name="finish",
    )(*final)
    bands = jax.ShapeDtypeStruct((3, 2, 9 * channels, 2 * channels), jnp.bfloat16)
    band1, band2 = pl.pallas_call(
        band_kernel,
        out_shape=(bands, bands),
        in_specs=[vmem(), vmem()],
        out_specs=(vmem(), vmem()),
        compiler_params=params(),
        name="bands",
    )(conv1_weight, conv2_weight)
    main = main.reshape(TX, TY, lanes)

    def moved(value, axis, count, step):
        pairs = [(i, i + step) for i in range(count) if 0 <= i + step < count]
        return lax.ppermute(value, axis, pairs)

    low = moved(last_rows.reshape(2, TY, lanes), "frames", n_frames, 1)
    high = moved(first_rows.reshape(2, TY, lanes), "frames", n_frames, -1)
    edge = jnp.concatenate([low[:, TY - 2 :], main[:, TY - 2 :], high[:, TY - 2 :]], axis=0)
    left = moved(edge, "rows", n_rows, 1)
    edge = jnp.concatenate([low[:, :2], main[:, :2], high[:, :2]], axis=0)
    right = moved(edge, "rows", n_rows, -1)
    ends = jnp.stack([f == 0, f == n_frames - 1, r == 0, r == n_rows - 1]).astype(jnp.int32)
    wide = 80
    out = pl.pallas_call(
        convolve_kernel,
        out_shape=jax.ShapeDtypeStruct((cells * DEPTH, channels), jnp.bfloat16),
        in_specs=[smem()] + [vmem()] * 9,
        out_specs=vmem(),
        scratch_shapes=[VMEM((TX + 4, wide, lanes), jnp.bfloat16)] * 3
        + [VMEM((TX + 2, wide, lanes), jnp.bfloat16)]
        + [VMEM((TX + 2, TY, lanes), jnp.bfloat16)] * 2
        + [VMEM((cells * DEPTH, channels), jnp.float32)],
        compiler_params=params(),
        name="convolve",
    )(ends, main, low, high, left, right, band1, band2, conv1_bias[None], conv2_bias[None])
    return out.reshape(TX, TY, DEPTH, channels)


def solution(mesh):
    placed = (
        P("frames", "rows", None, None),
        P("frames", "rows", None, None, None),
        P("frames", "rows", None),
        P("frames", "rows", None),
        P(),
        P(),
        P(),
        P(),
    )
    return jax.shard_map(
        shards,
        mesh=mesh,
        in_specs=placed,
        out_specs=P("frames", "rows", None, None),
        check_vma=False,
    )
```

```python
import functools

import jax
import jax.numpy as jnp
from jax import lax
from jax.experimental import pallas as pl
from jax.experimental.pallas import tpu as pltpu
from jax.sharding import PartitionSpec as P

DEPTH = 4
TX = 8
TY = 64
CORES = 2
PARTS = (1, 1, 1, 1)
LABEL_ROWS = 16
VMEM = pltpu.VMEM
LIMIT = 60 * 1024 * 1024


def vmem():
    return pl.BlockSpec(memory_space=pltpu.VMEM)


def smem():
    return pl.BlockSpec(memory_space=pltpu.SMEM)


def anywhere():
    return pl.BlockSpec(memory_space=pl.ANY)


def params():
    return pltpu.CompilerParams(vmem_limit_bytes=LIMIT)


def arrays(count, rows, channels, dtype=jnp.bfloat16):
    return [jax.ShapeDtypeStruct((rows, channels), dtype)] * count


def split_low(value, count):
    if count & (count - 1) == 0:
        return value >> (count.bit_length() - 1), value & (count - 1)
    return value // count, value % count


def apart(target, source, count):
    if count & (count - 1) == 0:
        return target ^ source
    return (target - source + count) % count


def step_to(source, step, count):
    if count & (count - 1) == 0:
        return source ^ step
    return (source + step) % count


def index_kernel(shape, slots, blocks, *refs):
    n_z, n_y, n_x, n_c = shape
    at_ref = refs[0]
    codes = refs[1 : 1 + n_c]
    index_ref, label_ref, counts, labels = refs[1 + n_c :]
    tiles = n_z * n_y * n_x * n_c
    groups = n_y * n_x
    spare = groups * n_z * slots

    def clear(t, carry):
        counts[t] = 0
        return carry

    lax.fori_loop(0, tiles, clear, 0, unroll=8)

    def blank(s, carry):
        labels[s] = -1
        return carry

    lax.fori_loop(0, spare, blank, 0, unroll=8)
    z, y, x, c = (at_ref[i] for i in range(4))
    pairs = codes[0].shape[0]
    for source in range(n_c):
        ref = codes[source]

        def place(p, carry):
            tile, block = split_low(ref[p], blocks)
            rank = counts[tile]
            counts[tile] = rank + 1
            rest, c_to = split_low(tile, n_c)
            rest, x_to = split_low(rest, n_x)
            z_to, y_to = split_low(rest, n_y)
            group = apart(y_to, y, n_y) * n_x + apart(x_to, x, n_x)
            slot = (group * n_z + apart(z_to, z, n_z)) * slots + rank
            slot = jnp.where(c_to == c, slot, spare)
            index_ref[source * pairs + p] = slot
            labels[slot] = block
            return carry

        lax.fori_loop(0, pairs, place, 0, unroll=4)
    lane = lax.broadcasted_iota(jnp.int32, (LABEL_ROWS, label_ref.shape[1]), 1)
    for g in range(groups):
        row = jnp.full(lane.shape, -1, jnp.int32)
        for k in range(n_z * slots):
            row = jnp.where(lane == k, labels[g * n_z * slots + k], row)
        label_ref[g * LABEL_ROWS : (g + 1) * LABEL_ROWS, :] = row.astype(jnp.float32).astype(jnp.bfloat16)


def contribute_kernel(n_c, groups, per_group, top, spans, first, *refs):
    index_ref = refs[0]
    sources = refs[1 : 1 + n_c]
    features = refs[1 + n_c : 1 + 2 * n_c]
    refs = refs[1 + 2 * n_c :]
    label_ref = refs[0]
    outs = refs[1 : 1 + groups * len(spans)]
    refs = refs[1 + groups * len(spans) :]
    buffers = refs[: len(spans)]
    held, load_sems, store_sems = refs[len(spans) :]
    images = features[0].shape[0]
    begin, rows = spans[0][0], sum(span[1] for span in spans)
    loads = [
        pltpu.make_async_copy(
            sources[s].at[:, pl.ds(begin, rows), :], held.at[pl.ds(s * images * top, images * top)], load_sems.at[s]
        )
        for s in range(n_c)
    ]
    for load in loads:
        load.start()
    for s in range(n_c):
        loads[s].wait()

        def image(b, carry):
            p0 = s * images * top + b * top
            weights = held[pl.ds(p0, top)].reshape(top * rows, held.shape[2])
            product = jnp.dot(weights, features[s][b], preferred_element_type=jnp.float32)
            product = product.astype(jnp.bfloat16)
            for t in range(top):
                slot = index_ref[p0 + t]
                for (start, chunk), buffer in zip(spans, buffers):
                    at = t * rows + start - begin
                    buffer[pl.ds(pl.multiple_of(slot * chunk, chunk), chunk), :] = product[at : at + chunk]
            return carry

        lax.fori_loop(0, images, image, 0, unroll=4)
    copies = []
    for i, ((_, chunk), buffer) in enumerate(zip(spans, buffers)):
        length = per_group * chunk
        for g in range(groups):
            n = i * groups + g
            data = outs[n].at[pl.ds(0, length)] if first else outs[n]
            copies.append(pltpu.make_async_copy(buffer.at[pl.ds(g * length, length)], data, store_sems.at[n]))
            if first:
                copies.append(
                    pltpu.make_async_copy(
                        label_ref.at[pl.ds(g * LABEL_ROWS, LABEL_ROWS)],
                        outs[n].at[pl.ds(length, LABEL_ROWS)],
                        store_sems.at[groups * len(spans) + g],
                    )
                )
    for copy in copies:
        copy.start()
    for copy in copies:
        copy.wait()


def merge_kernel(n_z, groups, slots, chunk, blocks, first, *refs):
    messages = refs[:groups]
    refs = refs[groups:]
    per_group = n_z * slots
    stride = per_group + 1
    if first:
        outs = refs[:n_z]
        plan_ref, total, marks, marks_smem, sem = refs[n_z:]
        for g in range(groups):
            row = messages[g][per_group * chunk :, :].astype(jnp.float32)
            marks[g : g + 1, :] = row[0:1, :].astype(jnp.int32)
        copy = pltpu.make_async_copy(marks, marks_smem, sem)
        copy.start()
    else:
        plan_ref = refs[0]
        outs = refs[2 : 2 + n_z]
        (total,) = refs[2 + n_z :]
    total[...] = jnp.zeros_like(total)
    if first:
        copy.wait()
        for g in range(groups):

            def note(s, count):
                label = marks_smem[g, s]
                plan_ref[g * stride + 1 + count] = s * blocks + jnp.maximum(label, 0)
                return count + (label >= 0).astype(jnp.int32)

            plan_ref[g * stride] = lax.fori_loop(0, per_group, note, 0, unroll=8)
    for g in range(groups):

        def add(n, carry):
            slot, label = split_low(plan_ref[g * stride + 1 + n], blocks)
            step = split_low(slot, slots)[0]
            source = pl.ds(pl.multiple_of(slot * chunk, chunk), chunk)
            target = pl.ds(pl.multiple_of((step * blocks + label) * chunk, chunk), chunk)
            total[target, :] += messages[g][source, :].astype(jnp.float32)
            return carry

        lax.fori_loop(0, plan_ref[g * stride], add, 0)
    rows = blocks * chunk
    for step, out in enumerate(outs):
        out[...] = total[step * rows : (step + 1) * rows, :].astype(jnp.bfloat16)


def finish_kernel(n_z, spans, blocks, size, *refs):
    count = n_z * len(spans)
    parts = refs[:count]
    out_ref, low_ref, high_ref, total = refs[count:]
    for k, (start, chunk) in enumerate(spans):
        for block in range(blocks):
            row = block * chunk
            value = None
            for ref in parts[k * n_z : (k + 1) * n_z]:
                part = ref[row : row + chunk, :].astype(jnp.float32)
                value = part if value is None else value + part
            at = block * size + start
            total[at : at + chunk, :] = value
    cells = total.shape[0] // DEPTH
    channels = total.shape[1]
    for z in range(DEPTH):
        part = total[pl.ds(z, cells, stride=DEPTH), :].astype(jnp.bfloat16)
        lanes = slice(z * channels, (z + 1) * channels)
        out_ref[:, lanes] = part
        low_ref[:, lanes] = part[: 2 * TY]
        high_ref[:, lanes] = part[cells - 2 * TY :]


def band_kernel(first_ref, second_ref, out1_ref, out2_ref):
    channels = first_ref.shape[-1]
    zero = jnp.zeros((channels, channels), jnp.bfloat16)
    for source, target in ((first_ref, out1_ref), (second_ref, out2_ref)):
        for dx in range(3):
            for half in range(2):
                for dy in range(3):
                    for k in range(3):
                        z_in = k + half
                        for j in range(2):
                            dz = z_in - (2 * half + j) + 1
                            value = source[dx, dy, dz] if 0 <= dz < 3 else zero
                            row = (dy * 3 + k) * channels
                            target[dx, half, row : row + channels, j * channels : (j + 1) * channels] = value


def convolve_half(copies, bands, half, out_rows, channels):
    total = None
    for dx in range(3):
        pieces = []
        for dy in range(3):
            piece = copies[dy][dx : dx + out_rows, :, half * channels : (half + 3) * channels]
            pieces.append(piece.reshape(-1, 3 * channels))
        product = jnp.dot(
            jnp.concatenate(pieces, axis=1), bands[dx, half], preferred_element_type=jnp.float32
        )
        total = product if total is None else total + product
    return total


def silu(v):
    return v / (1.0 + jnp.exp(-v))


def convolve_kernel(
    ends_ref, main_ref, low_ref, high_ref, left_ref, right_ref,
    band1_ref, band2_ref, bias1_ref, bias2_ref, out_ref,
    copies0, copies1, copies2, hidden, shift1, shift2, stage,
):
    channels = bias1_ref.shape[1]
    rows, cols = main_ref.shape[0], main_ref.shape[1]
    for x0, source in ((0, low_ref), (2, main_ref), (2 + rows, high_ref)):
        value = source[...]
        part = slice(x0, x0 + value.shape[0])
        copies0[part, 2 : 2 + cols, :] = value
        copies1[part, 1 : 1 + cols, :] = value
        copies2[part, 0:cols, :] = value
    left = left_ref[...]
    right = right_ref[...]
    copies0[:, 0:2, :] = left
    copies1[:, 0:1, :] = left[:, 1:2]
    copies1[:, 1 + cols : 2 + cols, :] = right[:, 0:1]
    copies2[:, cols : 2 + cols, :] = right
    for half in range(2):
        total = convolve_half((copies0, copies1, copies2), band1_ref, half, rows + 2, channels)
        bias = jnp.concatenate([bias1_ref[...], bias1_ref[...]], axis=1)
        value = silu(total + bias).reshape(rows + 2, -1, 2 * channels)
        x_at = lax.broadcasted_iota(jnp.int32, value.shape, 0)
        y_at = lax.broadcasted_iota(jnp.int32, value.shape, 1)
        keep = (x_at >= ends_ref[0]) & (x_at < rows + 2 - ends_ref[1])
        keep = keep & (y_at >= ends_ref[2]) & (y_at < cols + 2 - ends_ref[3])
        value = jnp.where(keep, value, 0.0).astype(jnp.bfloat16)
        hidden[:, :, half * 2 * channels : (half + 1) * 2 * channels] = value
    shift1[...] = hidden[:, 1 : 1 + cols, :]
    shift2[...] = hidden[:, 2 : 2 + cols, :]
    for half in range(2):
        total = convolve_half(
            (hidden.at[:, 0:cols, :], shift1, shift2), band2_ref, half, rows, channels
        )
        for j in range(2):
            value = silu(total[:, j * channels : (j + 1) * channels] + bias2_ref[...])
            stage[pl.ds(2 * half + j, rows * cols, stride=DEPTH), :] = value
    out_ref[...] = stage[...].astype(jnp.bfloat16)


def shards(features, pair_weight, target_tile, target_block, conv1_weight, conv1_bias, conv2_weight, conv2_bias):
    images, size, channels = features.shape[1:]
    top = target_tile.shape[2]
    n_frames = lax.axis_size("frames")
    n_rows = lax.axis_size("rows")
    devices = n_frames * n_rows
    capacity = max(2, 2 * images * top // devices)
    blocks = TX * TY * DEPTH // size
    n_c = CORES if n_rows % CORES == 0 else 1
    n_x = n_rows // n_c
    n_y = n_x if n_frames % n_x == 0 else 1
    n_z = n_frames // n_y
    shape = (n_z, n_y, n_x, n_c)
    groups = n_y * n_x
    slots = n_c * capacity
    per_group = n_z * slots
    stride = per_group + 1
    spans, start = [], 0
    for part in PARTS:
        spans.append((start * size // sum(PARTS), part * size // sum(PARTS)))
        start += part

    def moved_by(value, dz=0, dy=0, dx=0, dc=0):
        pairs = []
        for source in range(devices):
            f, r = divmod(source, n_rows)
            z, y = divmod(f, n_y)
            x, c = divmod(r, n_c)
            z, y, x = step_to(z, dz, n_z), step_to(y, dy, n_y), step_to(x, dx, n_x)
            c = step_to(c, dc, n_c)
            pairs.append((source, ((z * n_y + y) * n_x + x) * n_c + c))
        return lax.ppermute(value, ("frames", "rows"), pairs)

    f, r = lax.axis_index("frames"), lax.axis_index("rows")
    at = jnp.stack([f // n_y, f % n_y, r // n_c, r % n_c]).astype(jnp.int32)
    code = (target_tile * blocks + target_block).reshape(-1)
    weights = pair_weight[0].reshape(images * top, size, size)
    shared = [(weights, features[0], code)]
    for dc in range(1, n_c):
        shared.append(tuple(moved_by(v, dc=dc) for v in (weights, features[0], code)))
    index, labels = pl.pallas_call(
        functools.partial(index_kernel, shape, slots, blocks),
        out_shape=(
            jax.ShapeDtypeStruct((n_c * images * top,), jnp.int32),
            jax.ShapeDtypeStruct((groups * LABEL_ROWS, channels), jnp.bfloat16),
        ),
        in_specs=[smem()] * (1 + n_c),
        out_specs=(smem(), vmem()),
        scratch_shapes=[pltpu.SMEM((devices,), jnp.int32), pltpu.SMEM((groups * per_group + 1,), jnp.int32)],
        compiler_params=params(),
        name="index",
    )(at, *[v[2] for v in shared])

    def contribute(ks):
        own = [spans[k] for k in ks]
        first = ks[0] == 0
        outs, scratch = [], []
        for _, chunk in own:
            outs += arrays(groups, per_group * chunk + (LABEL_ROWS if first else 0), channels)
            scratch.append(VMEM(((groups * per_group + 1) * chunk, channels), jnp.bfloat16))
        rows = sum(chunk for _, chunk in own)
        scratch += [
            VMEM((n_c * images * top, rows, size), jnp.bfloat16),
            pltpu.SemaphoreType.DMA((n_c,)),
            pltpu.SemaphoreType.DMA((len(outs) + groups,)),
        ]
        made = pl.pallas_call(
            functools.partial(contribute_kernel, n_c, groups, per_group, top, own, first),
            out_shape=tuple(outs),
            in_specs=[smem()] + [anywhere()] * n_c + [vmem()] * (n_c + 1),
            out_specs=(anywhere(),) * len(outs),
            scratch_shapes=scratch,
            compiler_params=params(),
        )(index, *[v[0] for v in shared], *[v[1] for v in shared], labels)
        for i, k in enumerate(ks):
            messages[k] = made[i * groups : (i + 1) * groups]

    def exchange(k):
        return [
            moved_by(value, dy=g // n_x, dx=g % n_x) if g else value
            for g, value in enumerate(messages[k])
        ]

    def merge(k, received, plan, after):
        first = k == 0
        chunk = spans[k][1]
        outs = arrays(n_z, blocks * chunk, channels)
        out_specs = [vmem()] * n_z
        scratch = [VMEM((n_z * blocks * chunk, channels), jnp.float32)]
        in_specs = [vmem()] * groups
        args = tuple(received)
        if first:
            outs.append(jax.ShapeDtypeStruct((stride * groups,), jnp.int32))
            out_specs.append(smem())
            scratch += [
                VMEM((groups, channels), jnp.int32),
                pltpu.SMEM((groups, channels), jnp.int32),
                pltpu.SemaphoreType.DMA,
            ]
        else:
            in_specs += [smem(), anywhere()]
            args += (plan, after)
        return pl.pallas_call(
            functools.partial(merge_kernel, n_z, groups, slots, chunk, blocks, first),
            out_shape=tuple(outs),
            in_specs=in_specs,
            out_specs=tuple(out_specs),
            scratch_shapes=scratch,
            compiler_params=params(),
        )(*args)

    bands = jax.ShapeDtypeStruct((3, 2, 9 * channels, 2 * channels), jnp.bfloat16)
    band1, band2 = pl.pallas_call(
        band_kernel,
        out_shape=(bands, bands),
        in_specs=[vmem(), vmem()],
        out_specs=(vmem(), vmem()),
        compiler_params=params(),
        name="bands",
    )(conv1_weight, conv2_weight)
    messages = {}
    contribute([0])
    contribute(list(range(1, len(spans))))
    plan, final = None, []
    for k in range(len(spans)):
        merged = merge(k, exchange(k), plan, band1)
        if k == 0:
            plan = merged[-1]
        final += [moved_by(part, dz=dz) if dz else part for dz, part in enumerate(merged[:n_z])]
    cells = TX * TY
    lanes = DEPTH * channels
    main, first_rows, last_rows = pl.pallas_call(
        functools.partial(finish_kernel, n_z, spans, blocks, size),
        out_shape=(
            jax.ShapeDtypeStruct((cells, lanes), jnp.bfloat16),
            jax.ShapeDtypeStruct((2 * TY, lanes), jnp.bfloat16),
            jax.ShapeDtypeStruct((2 * TY, lanes), jnp.bfloat16),
        ),
        in_specs=[vmem()] * len(final),
        out_specs=(vmem(),) * 3,
        scratch_shapes=[VMEM((cells * DEPTH, channels), jnp.float32)],
        compiler_params=params(),
        name="finish",
    )(*final)
    main = main.reshape(TX, TY, lanes)

    def moved(value, axis, count, step):
        pairs = [(i, i + step) for i in range(count) if 0 <= i + step < count]
        return lax.ppermute(value, axis, pairs)

    low = moved(last_rows.reshape(2, TY, lanes), "frames", n_frames, 1)
    high = moved(first_rows.reshape(2, TY, lanes), "frames", n_frames, -1)
    edge = jnp.concatenate([low[:, TY - 2 :], main[:, TY - 2 :], high[:, TY - 2 :]], axis=0)
    left = moved(edge, "rows", n_rows, 1)
    edge = jnp.concatenate([low[:, :2], main[:, :2], high[:, :2]], axis=0)
    right = moved(edge, "rows", n_rows, -1)
    ends = jnp.stack([f == 0, f == n_frames - 1, r == 0, r == n_rows - 1]).astype(jnp.int32)
    wide = 80
    out = pl.pallas_call(
        convolve_kernel,
        out_shape=jax.ShapeDtypeStruct((cells * DEPTH, channels), jnp.bfloat16),
        in_specs=[smem()] + [vmem()] * 9,
        out_specs=vmem(),
        scratch_shapes=[VMEM((TX + 4, wide, lanes), jnp.bfloat16)] * 3
        + [VMEM((TX + 2, wide, lanes), jnp.bfloat16)]
        + [VMEM((TX + 2, TY, lanes), jnp.bfloat16)] * 2
        + [VMEM((cells * DEPTH, channels), jnp.float32)],
        compiler_params=params(),
        name="convolve",
    )(ends, main, low, high, left, right, band1, band2, conv1_bias[None], conv2_bias[None])
    return out.reshape(TX, TY, DEPTH, channels)


def solution(mesh):
    placed = (
        P("frames", "rows", None, None),
        P("frames", "rows", None, None, None),
        P("frames", "rows", None),
        P("frames", "rows", None),
        P(),
        P(),
        P(),
        P(),
    )
    return jax.shard_map(
        shards,
        mesh=mesh,
        in_specs=placed,
        out_specs=P("frames", "rows", None, None),
        check_vma=False,
    )
```

```python
import functools

import jax
import jax.numpy as jnp
from jax import lax
from jax.experimental import pallas as pl
from jax.experimental.pallas import tpu as pltpu
from jax.sharding import PartitionSpec as P


DEPTH = 4
TX = 8
TY = 64
CORES = 2
PARTS = (1, 1, 1, 1)
LABEL_ROWS = 16
VMEM = pltpu.VMEM
LIMIT = 20 * 1024 * 1024


def vmem():
    return pl.BlockSpec(memory_space=pltpu.VMEM)


def smem():
    return pl.BlockSpec(memory_space=pltpu.SMEM)


def anywhere():
    return pl.BlockSpec(memory_space=pl.ANY)


def params():
    return pltpu.CompilerParams(vmem_limit_bytes=LIMIT)


def arrays(count, rows, channels, dtype=jnp.bfloat16):
    return [jax.ShapeDtypeStruct((rows, channels), dtype)] * count


def split_low(value, count):
    if count & (count - 1) == 0:
        return value >> (count.bit_length() - 1), value & (count - 1)
    return value // count, value % count


def apart(target, source, count):
    if count & (count - 1) == 0:
        return target ^ source
    return (target - source + count) % count


def step_to(source, step, count):
    if count & (count - 1) == 0:
        return source ^ step
    return (source + step) % count


def index_kernel(shape, slots, blocks, *refs):
    n_z, n_y, n_x, n_c = shape
    at_ref = refs[0]
    codes = refs[1 : 1 + n_c]
    index_ref, label_ref, counts, labels = refs[1 + n_c :]
    tiles = n_z * n_y * n_x * n_c
    groups = n_y * n_x
    spare = groups * n_z * slots

    def clear(t, carry):
        counts[t] = 0
        return carry

    lax.fori_loop(0, tiles, clear, 0, unroll=8)

    def blank(s, carry):
        labels[s] = -1
        return carry

    lax.fori_loop(0, spare, blank, 0, unroll=8)
    z, y, x, c = (at_ref[i] for i in range(4))
    pairs = codes[0].shape[0]
    for source in range(n_c):
        ref = codes[source]

        def place(p, carry):
            tile, block = split_low(ref[p], blocks)
            rank = counts[tile]
            counts[tile] = rank + 1
            rest, c_to = split_low(tile, n_c)
            rest, x_to = split_low(rest, n_x)
            z_to, y_to = split_low(rest, n_y)
            group = apart(y_to, y, n_y) * n_x + apart(x_to, x, n_x)
            slot = (group * n_z + apart(z_to, z, n_z)) * slots + rank
            slot = jnp.where(c_to == c, slot, spare)
            index_ref[source * pairs + p] = slot
            labels[slot] = block
            return carry

        lax.fori_loop(0, pairs, place, 0, unroll=4)
    lane = lax.broadcasted_iota(jnp.int32, (LABEL_ROWS, label_ref.shape[1]), 1)
    for g in range(groups):
        row = jnp.full(lane.shape, -1, jnp.int32)
        for k in range(n_z * slots):
            row = jnp.where(lane == k, labels[g * n_z * slots + k], row)
        label_ref[g * LABEL_ROWS : (g + 1) * LABEL_ROWS, :] = row.astype(jnp.float32).astype(jnp.bfloat16)


def contribute_kernel(n_c, groups, per_group, top, spans, first, *refs):
    index_ref = refs[0]
    sources = refs[1 : 1 + n_c]
    features = refs[1 + n_c : 1 + 2 * n_c]
    refs = refs[1 + 2 * n_c :]
    label_ref = refs[0]
    outs = refs[1 : 1 + groups * len(spans)]
    refs = refs[1 + groups * len(spans) :]
    buffers = refs[: len(spans)]
    held, load_sems, store_sems = refs[len(spans) :]
    images = features[0].shape[0]
    begin, rows = spans[0][0], sum(span[1] for span in spans)
    loads = [
        pltpu.make_async_copy(
            sources[s].at[:, pl.ds(begin, rows), :], held.at[pl.ds(s * images * top, images * top)], load_sems.at[s]
        )
        for s in range(n_c)
    ]
    for load in loads:
        load.start()
    for s in range(n_c):
        loads[s].wait()

        def image(b, carry):
            p0 = s * images * top + b * top
            weights = held[pl.ds(p0, top)].reshape(top * rows, held.shape[2])
            product = jnp.dot(weights, features[s][b], preferred_element_type=jnp.float32)
            product = product.astype(jnp.bfloat16)
            for t in range(top):
                slot = index_ref[p0 + t]
                for (start, chunk), buffer in zip(spans, buffers):
                    at = t * rows + start - begin
                    buffer[pl.ds(pl.multiple_of(slot * chunk, chunk), chunk), :] = product[at : at + chunk]
            return carry

        lax.fori_loop(0, images, image, 0, unroll=4)
    copies = []
    for i, ((_, chunk), buffer) in enumerate(zip(spans, buffers)):
        length = per_group * chunk
        for g in range(groups):
            n = i * groups + g
            data = outs[n].at[pl.ds(0, length)] if first else outs[n]
            copies.append(pltpu.make_async_copy(buffer.at[pl.ds(g * length, length)], data, store_sems.at[n]))
            if first:
                copies.append(
                    pltpu.make_async_copy(
                        label_ref.at[pl.ds(g * LABEL_ROWS, LABEL_ROWS)],
                        outs[n].at[pl.ds(length, LABEL_ROWS)],
                        store_sems.at[groups * len(spans) + g],
                    )
                )
    for copy in copies:
        copy.start()
    for copy in copies:
        copy.wait()


def merge_kernel(n_z, groups, slots, chunk, blocks, first, *refs):
    messages = refs[:groups]
    refs = refs[groups:]
    per_group = n_z * slots
    stride = per_group + 1
    if first:
        outs = refs[:n_z]
        plan_ref, total, marks, marks_smem, sem = refs[n_z:]
        for g in range(groups):
            row = messages[g][per_group * chunk :, :].astype(jnp.float32)
            marks[g : g + 1, :] = row[0:1, :].astype(jnp.int32)
        copy = pltpu.make_async_copy(marks, marks_smem, sem)
        copy.start()
    else:
        plan_ref = refs[0]
        outs = refs[1 : 1 + n_z]
        (total,) = refs[1 + n_z :]
    total[...] = jnp.zeros_like(total)
    if first:
        copy.wait()
        for g in range(groups):

            def note(s, count):
                label = marks_smem[g, s]
                plan_ref[g * stride + 1 + count] = s * blocks + jnp.maximum(label, 0)
                return count + (label >= 0).astype(jnp.int32)

            plan_ref[g * stride] = lax.fori_loop(0, per_group, note, 0, unroll=8)
    for g in range(groups):

        def add(n, carry):
            slot, label = split_low(plan_ref[g * stride + 1 + n], blocks)
            step = split_low(slot, slots)[0]
            source = pl.ds(pl.multiple_of(slot * chunk, chunk), chunk)
            target = pl.ds(pl.multiple_of((step * blocks + label) * chunk, chunk), chunk)
            total[target, :] += messages[g][source, :].astype(jnp.float32)
            return carry

        lax.fori_loop(0, plan_ref[g * stride], add, 0)
    rows = blocks * chunk
    for step, out in enumerate(outs):
        out[...] = total[step * rows : (step + 1) * rows, :].astype(jnp.bfloat16)


def finish_kernel(n_z, spans, blocks, size, *refs):
    count = n_z * len(spans)
    parts = refs[:count]
    out_ref, low_ref, high_ref, total = refs[count + 1 :]
    for k, (start, chunk) in enumerate(spans):
        for block in range(blocks):
            row = block * chunk
            value = None
            for ref in parts[k * n_z : (k + 1) * n_z]:
                part = ref[row : row + chunk, :].astype(jnp.float32)
                value = part if value is None else value + part
            at = block * size + start
            total[at : at + chunk, :] = value
    cells = total.shape[0] // DEPTH
    channels = total.shape[1]
    for z in range(DEPTH):
        part = total[pl.ds(z, cells, stride=DEPTH), :].astype(jnp.bfloat16)
        lanes = slice(z * channels, (z + 1) * channels)
        out_ref[:, lanes] = part
        low_ref[:, lanes] = part[: 2 * TY]
        high_ref[:, lanes] = part[cells - 2 * TY :]


def band_kernel(first_ref, second_ref, after_ref, out1_ref, out2_ref):
    channels = first_ref.shape[-1]
    zero = jnp.zeros((channels, channels), jnp.bfloat16)
    for source, target in ((first_ref, out1_ref), (second_ref, out2_ref)):
        for dx in range(3):
            for half in range(2):
                for dy in range(3):
                    for k in range(3):
                        z_in = k + half
                        for j in range(2):
                            dz = z_in - (2 * half + j) + 1
                            value = source[dx, dy, dz] if 0 <= dz < 3 else zero
                            row = (dy * 3 + k) * channels
                            target[dx, half, row : row + channels, j * channels : (j + 1) * channels] = value


def convolve_half(copies, bands, half, out_rows, channels):
    total = None
    for dx in range(3):
        pieces = []
        for dy in range(3):
            piece = copies[dy][dx : dx + out_rows, :, half * channels : (half + 3) * channels]
            pieces.append(piece.reshape(-1, 3 * channels))
        product = jnp.dot(
            jnp.concatenate(pieces, axis=1), bands[dx, half], preferred_element_type=jnp.float32
        )
        total = product if total is None else total + product
    return total


def silu(v):
    return v / (1.0 + jnp.exp(-v))


def convolve_kernel(
    ends_ref, main_ref, low_ref, high_ref, left_ref, right_ref,
    band1_ref, band2_ref, bias1_ref, bias2_ref, out_ref,
    copies0, copies1, copies2, hidden, shift1, shift2, stage,
):
    channels = bias1_ref.shape[1]
    rows, cols = main_ref.shape[0], main_ref.shape[1]
    for x0, source in ((0, low_ref), (2, main_ref), (2 + rows, high_ref)):
        value = source[...]
        part = slice(x0, x0 + value.shape[0])
        copies0[part, 2 : 2 + cols, :] = value
        copies1[part, 1 : 1 + cols, :] = value
        copies2[part, 0:cols, :] = value
    left = left_ref[...]
    right = right_ref[...]
    copies0[:, 0:2, :] = left
    copies1[:, 0:1, :] = left[:, 1:2]
    copies1[:, 1 + cols : 2 + cols, :] = right[:, 0:1]
    copies2[:, cols : 2 + cols, :] = right
    for half in range(2):
        total = convolve_half((copies0, copies1, copies2), band1_ref, half, rows + 2, channels)
        bias = jnp.concatenate([bias1_ref[...], bias1_ref[...]], axis=1)
        value = silu(total + bias).reshape(rows + 2, -1, 2 * channels)
        x_at = lax.broadcasted_iota(jnp.int32, value.shape, 0)
        y_at = lax.broadcasted_iota(jnp.int32, value.shape, 1)
        keep = (x_at >= ends_ref[0]) & (x_at < rows + 2 - ends_ref[1])
        keep = keep & (y_at >= ends_ref[2]) & (y_at < cols + 2 - ends_ref[3])
        value = jnp.where(keep, value, 0.0).astype(jnp.bfloat16)
        hidden[:, :, half * 2 * channels : (half + 1) * 2 * channels] = value
    shift1[...] = hidden[:, 1 : 1 + cols, :]
    shift2[...] = hidden[:, 2 : 2 + cols, :]
    for half in range(2):
        total = convolve_half(
            (hidden.at[:, 0:cols, :], shift1, shift2), band2_ref, half, rows, channels
        )
        for j in range(2):
            value = silu(total[:, j * channels : (j + 1) * channels] + bias2_ref[...])
            stage[pl.ds(2 * half + j, rows * cols, stride=DEPTH), :] = value
    out_ref[...] = stage[...].astype(jnp.bfloat16)


def shards(features, pair_weight, target_tile, target_block, conv1_weight, conv1_bias, conv2_weight, conv2_bias):
    images, size, channels = features.shape[1:]
    top = target_tile.shape[2]
    n_frames = lax.axis_size("frames")
    n_rows = lax.axis_size("rows")
    devices = n_frames * n_rows
    capacity = max(2, 2 * images * top // devices)
    blocks = TX * TY * DEPTH // size
    n_c = CORES if n_rows % CORES == 0 else 1
    n_x = n_rows // n_c
    n_y = n_x if n_frames % n_x == 0 else 1
    n_z = n_frames // n_y
    shape = (n_z, n_y, n_x, n_c)
    groups = n_y * n_x
    slots = n_c * capacity
    per_group = n_z * slots
    stride = per_group + 1
    spans, start = [], 0
    for part in PARTS:
        spans.append((start * size // sum(PARTS), part * size // sum(PARTS)))
        start += part

    def moved_by(value, dz=0, dy=0, dx=0, dc=0):
        pairs = []
        for source in range(devices):
            f, r = divmod(source, n_rows)
            z, y = divmod(f, n_y)
            x, c = divmod(r, n_c)
            z, y, x = step_to(z, dz, n_z), step_to(y, dy, n_y), step_to(x, dx, n_x)
            c = step_to(c, dc, n_c)
            pairs.append((source, ((z * n_y + y) * n_x + x) * n_c + c))
        return lax.ppermute(value, ("frames", "rows"), pairs)

    f, r = lax.axis_index("frames"), lax.axis_index("rows")
    at = jnp.stack([f // n_y, f % n_y, r // n_c, r % n_c]).astype(jnp.int32)
    code = (target_tile * blocks + target_block).reshape(-1)
    weights = pair_weight[0].reshape(images * top, size, size)
    shared = [(weights, features[0], code)]
    for dc in range(1, n_c):
        shared.append(tuple(moved_by(v, dc=dc) for v in (weights, features[0], code)))
    index, labels = pl.pallas_call(
        functools.partial(index_kernel, shape, slots, blocks),
        out_shape=(
            jax.ShapeDtypeStruct((n_c * images * top,), jnp.int32),
            jax.ShapeDtypeStruct((groups * LABEL_ROWS, channels), jnp.bfloat16),
        ),
        in_specs=[smem()] * (1 + n_c),
        out_specs=(smem(), vmem()),
        scratch_shapes=[pltpu.SMEM((devices,), jnp.int32), pltpu.SMEM((groups * per_group + 1,), jnp.int32)],
        compiler_params=params(),
        name="index",
    )(at, *[v[2] for v in shared])

    def contribute(ks):
        own = [spans[k] for k in ks]
        first = ks[0] == 0
        outs, scratch = [], []
        for _, chunk in own:
            outs += arrays(groups, per_group * chunk + (LABEL_ROWS if first else 0), channels)
            scratch.append(VMEM(((groups * per_group + 1) * chunk, channels), jnp.bfloat16))
        rows = sum(chunk for _, chunk in own)
        scratch += [
            VMEM((n_c * images * top, rows, size), jnp.bfloat16),
            pltpu.SemaphoreType.DMA((n_c,)),
            pltpu.SemaphoreType.DMA((len(outs) + groups,)),
        ]
        made = pl.pallas_call(
            functools.partial(contribute_kernel, n_c, groups, per_group, top, own, first),
            out_shape=tuple(outs),
            in_specs=[smem()] + [anywhere()] * n_c + [vmem()] * (n_c + 1),
            out_specs=(anywhere(),) * len(outs),
            scratch_shapes=scratch,
            compiler_params=params(),
        )(index, *[v[0] for v in shared], *[v[1] for v in shared], labels)
        for i, k in enumerate(ks):
            messages[k] = made[i * groups : (i + 1) * groups]

    def exchange(k):
        return [
            moved_by(value, dy=g // n_x, dx=g % n_x) if g else value
            for g, value in enumerate(messages[k])
        ]

    def merge(k, received, plan):
        first = k == 0
        chunk = spans[k][1]
        outs = arrays(n_z, blocks * chunk, channels)
        out_specs = [vmem()] * n_z
        scratch = [VMEM((n_z * blocks * chunk, channels), jnp.float32)]
        in_specs = [vmem()] * groups
        args = tuple(received)
        if first:
            outs.append(jax.ShapeDtypeStruct((stride * groups,), jnp.int32))
            out_specs.append(smem())
            scratch += [
                VMEM((groups, channels), jnp.int32),
                pltpu.SMEM((groups, channels), jnp.int32),
                pltpu.SemaphoreType.DMA,
            ]
        else:
            in_specs.append(smem())
            args += (plan,)
        return pl.pallas_call(
            functools.partial(merge_kernel, n_z, groups, slots, chunk, blocks, first),
            out_shape=tuple(outs),
            in_specs=in_specs,
            out_specs=tuple(out_specs),
            scratch_shapes=scratch,
            compiler_params=params(),
        )(*args)

    messages = {}
    contribute([0])
    contribute(list(range(1, len(spans))))
    plan, final = None, []
    for k in range(len(spans)):
        merged = merge(k, exchange(k), plan)
        if k == 0:
            plan = merged[-1]
        final += [moved_by(part, dz=dz) if dz else part for dz, part in enumerate(merged[:n_z])]
    bands = jax.ShapeDtypeStruct((3, 2, 9 * channels, 2 * channels), jnp.bfloat16)
    band1, band2 = pl.pallas_call(
        band_kernel,
        out_shape=(bands, bands),
        in_specs=[vmem(), vmem(), anywhere()],
        out_specs=(vmem(), vmem()),
        compiler_params=params(),
        name="bands",
    )(conv1_weight, conv2_weight, merged[0])
    cells = TX * TY
    lanes = DEPTH * channels
    main, first_rows, last_rows = pl.pallas_call(
        functools.partial(finish_kernel, n_z, spans, blocks, size),
        out_shape=(
            jax.ShapeDtypeStruct((cells, lanes), jnp.bfloat16),
            jax.ShapeDtypeStruct((2 * TY, lanes), jnp.bfloat16),
            jax.ShapeDtypeStruct((2 * TY, lanes), jnp.bfloat16),
        ),
        in_specs=[vmem()] * len(final) + [anywhere()],
        out_specs=(vmem(),) * 3,
        scratch_shapes=[VMEM((cells * DEPTH, channels), jnp.float32)],
        compiler_params=params(),
        name="finish",
    )(*final, band1)
    main = main.reshape(TX, TY, lanes)

    def moved(value, axis, count, step):
        pairs = [(i, i + step) for i in range(count) if 0 <= i + step < count]
        return lax.ppermute(value, axis, pairs)

    low = moved(last_rows.reshape(2, TY, lanes), "frames", n_frames, 1)
    high = moved(first_rows.reshape(2, TY, lanes), "frames", n_frames, -1)
    edge = jnp.concatenate([low[:, TY - 2 :], main[:, TY - 2 :], high[:, TY - 2 :]], axis=0)
    left = moved(edge, "rows", n_rows, 1)
    edge = jnp.concatenate([low[:, :2], main[:, :2], high[:, :2]], axis=0)
    right = moved(edge, "rows", n_rows, -1)
    ends = jnp.stack([f == 0, f == n_frames - 1, r == 0, r == n_rows - 1]).astype(jnp.int32)
    wide = 80
    out = pl.pallas_call(
        convolve_kernel,
        out_shape=jax.ShapeDtypeStruct((cells * DEPTH, channels), jnp.bfloat16),
        in_specs=[smem()] + [vmem()] * 9,
        out_specs=vmem(),
        scratch_shapes=[VMEM((TX + 4, wide, lanes), jnp.bfloat16)] * 3
        + [VMEM((TX + 2, wide, lanes), jnp.bfloat16)]
        + [VMEM((TX + 2, TY, lanes), jnp.bfloat16)] * 2
        + [VMEM((cells * DEPTH, channels), jnp.float32)],
        compiler_params=params(),
        name="convolve",
    )(ends, main, low, high, left, right, band1, band2, conv1_bias[None], conv2_bias[None])
    return out.reshape(TX, TY, DEPTH, channels)


def solution(mesh):
    placed = (
        P("frames", "rows", None, None),
        P("frames", "rows", None, None, None),
        P("frames", "rows", None),
        P("frames", "rows", None),
        P(),
        P(),
        P(),
        P(),
    )
    return jax.shard_map(
        shards,
        mesh=mesh,
        in_specs=placed,
        out_specs=P("frames", "rows", None, None),
        check_vma=False,
    )
```

```python
import functools

import jax
import jax.numpy as jnp
from jax import lax
from jax.experimental import pallas as pl
from jax.experimental.pallas import tpu as pltpu
from jax.sharding import PartitionSpec as P


DEPTH = 4
TX = 8
TY = 64
CORES = 2
ORDER = (0, 3, 1, 2)
LABEL_ROWS = 16
VMEM = pltpu.VMEM
LIMIT = 12 * 1024 * 1024


def vmem():
    return pl.BlockSpec(memory_space=pltpu.VMEM)


def smem():
    return pl.BlockSpec(memory_space=pltpu.SMEM)


def anywhere():
    return pl.BlockSpec(memory_space=pl.ANY)


def params():
    return pltpu.CompilerParams(vmem_limit_bytes=LIMIT)


def arrays(count, rows, channels, dtype=jnp.bfloat16):
    return [jax.ShapeDtypeStruct((rows, channels), dtype)] * count


def split_low(value, count):
    if count & (count - 1) == 0:
        return value >> (count.bit_length() - 1), value & (count - 1)
    return value // count, value % count


def apart(target, source, count):
    if count & (count - 1) == 0:
        return target ^ source
    return (target - source + count) % count


def step_to(source, step, count):
    if count & (count - 1) == 0:
        return source ^ step
    return (source + step) % count


def index_kernel(shape, slots, blocks, *refs):
    n_z, n_y, n_x, n_c = shape
    codes = refs[:n_c]
    weight_ref, feature_ref, index_ref, label_ref, weight_out, feature_out, counts, labels, sems = refs[n_c:]
    copies = [
        pltpu.make_async_copy(feature_ref, feature_out, sems.at[0]),
        pltpu.make_async_copy(weight_ref, weight_out, sems.at[1]),
    ]
    for copy in copies:
        copy.start()
    tiles = n_z * n_y * n_x * n_c
    groups = n_y * n_x
    spare = groups * n_z * slots

    def clear(t, carry):
        counts[t] = 0
        return carry

    lax.fori_loop(0, tiles, clear, 0, unroll=8)

    def blank(s, carry):
        labels[s] = -1
        return carry

    lax.fori_loop(0, spare, blank, 0, unroll=8)
    z, y = split_low(lax.axis_index("frames"), n_y)
    x, c = split_low(lax.axis_index("rows"), n_c)
    pairs = codes[0].shape[0]
    for source in range(n_c):
        ref = codes[source]

        def place(p, carry):
            tile, block = split_low(ref[p], blocks)
            rank = counts[tile]
            counts[tile] = rank + 1
            rest, c_to = split_low(tile, n_c)
            rest, x_to = split_low(rest, n_x)
            z_to, y_to = split_low(rest, n_y)
            group = apart(y_to, y, n_y) * n_x + apart(x_to, x, n_x)
            slot = (group * n_z + apart(z_to, z, n_z)) * slots + rank
            slot = jnp.where(c_to == c, slot, spare)
            index_ref[source * pairs + p] = slot
            labels[slot] = block
            return carry

        lax.fori_loop(0, pairs, place, 0, unroll=4)
    lane = lax.broadcasted_iota(jnp.int32, (LABEL_ROWS, label_ref.shape[1]), 1)
    for g in range(groups):
        row = jnp.full(lane.shape, -1, jnp.int32)
        for k in range(n_z * slots):
            row = jnp.where(lane == k, labels[g * n_z * slots + k], row)
        label_ref[g * LABEL_ROWS : (g + 1) * LABEL_ROWS, :] = row.astype(jnp.float32).astype(jnp.bfloat16)
    for copy in copies:
        copy.wait()


def contribute_kernel(n_c, groups, per_group, top, spans, first, *refs):
    index_ref = refs[0]
    sources = refs[1 : 1 + n_c]
    features = refs[1 + n_c : 1 + 2 * n_c]
    refs = refs[1 + 2 * n_c :]
    label_ref = refs[0]
    outs = refs[1 : 1 + groups * len(spans)]
    refs = refs[1 + groups * len(spans) :]
    buffers = refs[: len(spans)]
    held, load_sems, store_sems = refs[len(spans) :]
    images = features[0].shape[0]
    begin, rows = min(span[0] for span in spans), sum(span[1] for span in spans)
    loads = [
        pltpu.make_async_copy(
            sources[s].at[:, pl.ds(begin, rows), :], held.at[pl.ds(s * images * top, images * top)], load_sems.at[s]
        )
        for s in range(n_c)
    ]
    for load in loads:
        load.start()
    for s in range(n_c):
        loads[s].wait()

        def image(b, carry):
            p0 = s * images * top + b * top
            weights = held[pl.ds(p0, top)].reshape(top * rows, held.shape[2])
            product = jnp.dot(weights, features[s][b], preferred_element_type=jnp.float32)
            product = product.astype(jnp.bfloat16)
            for t in range(top):
                slot = index_ref[p0 + t]
                for (start, chunk), buffer in zip(spans, buffers):
                    at = t * rows + start - begin
                    buffer[pl.ds(pl.multiple_of(slot * chunk, chunk), chunk), :] = product[at : at + chunk]
            return carry

        lax.fori_loop(0, images, image, 0, unroll=4)
    copies = []
    for i, ((_, chunk), buffer) in enumerate(zip(spans, buffers)):
        length = per_group * chunk
        for g in range(groups):
            n = i * groups + g
            data = outs[n].at[pl.ds(0, length)] if first else outs[n]
            copies.append(pltpu.make_async_copy(buffer.at[pl.ds(g * length, length)], data, store_sems.at[n]))
            if first:
                copies.append(
                    pltpu.make_async_copy(
                        label_ref.at[pl.ds(g * LABEL_ROWS, LABEL_ROWS)],
                        outs[n].at[pl.ds(length, LABEL_ROWS)],
                        store_sems.at[groups * len(spans) + g],
                    )
                )
    for copy in copies:
        copy.start()
    for copy in copies:
        copy.wait()


def merge_kernel(n_z, groups, slots, chunk, blocks, first, *refs):
    messages = refs[:groups]
    refs = refs[groups:]
    per_group = n_z * slots
    stride = per_group + 1
    if first:
        outs = refs[:n_z]
        plan_ref, total, marks, marks_smem, sem = refs[n_z:]
        for g in range(groups):
            row = messages[g][per_group * chunk :, :].astype(jnp.float32)
            marks[g : g + 1, :] = row[0:1, :].astype(jnp.int32)
        copy = pltpu.make_async_copy(marks, marks_smem, sem)
        copy.start()
    else:
        plan_ref = refs[0]
        outs = refs[1 : 1 + n_z]
        (total,) = refs[1 + n_z :]
    total[...] = jnp.zeros_like(total)
    if first:
        copy.wait()
        for g in range(groups):

            def note(s, count):
                label = marks_smem[g, s]
                plan_ref[g * stride + 1 + count] = s * blocks + jnp.maximum(label, 0)
                return count + (label >= 0).astype(jnp.int32)

            plan_ref[g * stride] = lax.fori_loop(0, per_group, note, 0, unroll=8)
    for g in range(groups):

        def add(n, carry):
            slot, label = split_low(plan_ref[g * stride + 1 + n], blocks)
            step = split_low(slot, slots)[0]
            source = pl.ds(pl.multiple_of(slot * chunk, chunk), chunk)
            target = pl.ds(pl.multiple_of((step * blocks + label) * chunk, chunk), chunk)
            total[target, :] += messages[g][source, :].astype(jnp.float32)
            return carry

        lax.fori_loop(0, plan_ref[g * stride], add, 0)
    rows = blocks * chunk
    for step, out in enumerate(outs):
        out[...] = total[step * rows : (step + 1) * rows, :].astype(jnp.bfloat16)


def sum_parts(parts, block, chunk):
    value = None
    for ref in parts:
        part = ref[block * chunk : (block + 1) * chunk, :].astype(jnp.float32)
        value = part if value is None else value + part
    return value


def tail_kernel(n_z, blocks, halves, *refs):
    parts = refs[: 2 * n_z]
    left_ref, right_ref, columns = refs[2 * n_z + 1 :]
    chunk = parts[0].shape[0] // blocks
    width = 2 * DEPTH
    channels = columns.shape[2]
    for x in range(blocks // halves):
        value = sum_parts(parts[:n_z], x * halves, chunk)
        columns[0, x * width : (x + 1) * width, :] = value[:width]
        value = sum_parts(parts[n_z:], x * halves + halves - 1, chunk)
        columns[1, x * width : (x + 1) * width, :] = value[chunk - width :]
    cells = columns.shape[1] // DEPTH
    for side, ref in enumerate((left_ref, right_ref)):
        for z in range(DEPTH):
            part = columns[side, pl.ds(z, cells, stride=DEPTH), :].astype(jnp.bfloat16)
            ref[:, z * channels : (z + 1) * channels] = part


def finish_kernel(n_z, spans, blocks, size, *refs):
    count = n_z * len(spans)
    parts = refs[:count]
    left_ref, right_ref, _, out_ref, first_ref, last_ref, total = refs[count:]
    for k, (start, chunk) in enumerate(spans):
        for block in range(blocks):
            at = block * size + start
            total[at : at + chunk, :] = sum_parts(parts[k * n_z : (k + 1) * n_z], block, chunk)
    cells = total.shape[0] // DEPTH
    channels = total.shape[1]
    for z in range(DEPTH):
        part = total[pl.ds(z, cells, stride=DEPTH), :].astype(jnp.bfloat16)
        lanes = slice(z * channels, (z + 1) * channels)
        out_ref[:, lanes] = part
        for x in range(2):
            first_ref[x, 0:TY, lanes] = part[x * TY : (x + 1) * TY]
            last_ref[x, 0:TY, lanes] = part[cells - (2 - x) * TY : cells - (1 - x) * TY]
    rows = cells // TY
    for x in range(2):
        for ref, at in ((first_ref, x), (last_ref, rows - 2 + x)):
            ref[x, TY : TY + 2, :] = left_ref[2 * at : 2 * at + 2, :]
            ref[x, TY + 2 : TY + 4, :] = right_ref[2 * at : 2 * at + 2, :]


def band_kernel(first_ref, second_ref, after_ref, out1_ref, out2_ref):
    channels = first_ref.shape[-1]
    zero = jnp.zeros((channels, channels), jnp.bfloat16)
    for source, target in ((first_ref, out1_ref), (second_ref, out2_ref)):
        for dx in range(3):
            for half in range(2):
                for dy in range(3):
                    for k in range(3):
                        z_in = k + half
                        for j in range(2):
                            dz = z_in - (2 * half + j) + 1
                            value = source[dx, dy, dz] if 0 <= dz < 3 else zero
                            row = (dy * 3 + k) * channels
                            target[dx, half, row : row + channels, j * channels : (j + 1) * channels] = value


def silu(v):
    return v / (1.0 + jnp.exp(-v))


def convolve_half(copies, bands, half, slabs, out_rows, channels):
    total = None
    for dx in range(3):
        pieces = []
        for dy in range(3):
            lanes = slice(half * channels, (half + 3) * channels)
            height = copies[dy].shape[0] // slabs
            parts = [copies[dy][s * height + dx : s * height + dx + out_rows, :, lanes] for s in range(slabs)]
            piece = parts[0] if slabs == 1 else jnp.concatenate(parts, axis=0)
            pieces.append(piece.reshape(-1, 3 * channels))
        product = jnp.dot(
            jnp.concatenate(pieces, axis=1), bands[dx, half], preferred_element_type=jnp.float32
        )
        total = product if total is None else total + product
    return total


def volume_ends():
    ends = []
    for axis in ("frames", "rows"):
        at = lax.axis_index(axis)
        ends += [(at == 0).astype(jnp.int32), (at == lax.axis_size(axis) - 1).astype(jnp.int32)]
    return ends


def first_layer(copies, band_ref, bias_ref, slabs, out_rows, cols, put):
    ends = volume_ends()
    channels = bias_ref.shape[1]
    bias = jnp.concatenate([bias_ref[...], bias_ref[...]], axis=1)
    for half in range(2):
        total = convolve_half(copies, band_ref, half, slabs, out_rows, channels)
        value = silu(total + bias).reshape(slabs * out_rows, -1, 2 * channels)
        y_at = lax.broadcasted_iota(jnp.int32, value.shape, 1)
        keep = (y_at >= ends[2]) & (y_at < cols + 2 - ends[3])
        if slabs > 1:
            x_at = lax.broadcasted_iota(jnp.int32, value.shape, 0)
            keep = keep & (x_at >= ends[0]) & (x_at < slabs * out_rows - ends[1])
        value = jnp.where(keep, value, 0.0).astype(jnp.bfloat16)
        put(half, value)


def second_layer(copies, band_ref, bias_ref, slabs, out_rows, stage):
    channels = bias_ref.shape[1]
    cells = stage.shape[0] // DEPTH
    for half in range(2):
        total = convolve_half(copies, band_ref, half, slabs, out_rows, channels)
        for j in range(2):
            value = silu(total[:, j * channels : (j + 1) * channels] + bias_ref[...])
            stage[pl.ds(2 * half + j, cells, stride=DEPTH), :] = value


def fill(copies, x0, value, left, right):
    cols = value.shape[1]
    part = slice(x0, x0 + value.shape[0])
    copies[0][part, 2 : 2 + cols, :] = value
    copies[1][part, 1 : 1 + cols, :] = value
    copies[2][part, 0:cols, :] = value
    for i in range(value.shape[0]):
        x, j = x0 + i, 2 * i
        copies[0][x, 0:2, :] = left[j : j + 2]
        copies[1][x, 0:1, :] = left[j + 1 : j + 2]
        copies[1][x, 1 + cols : 2 + cols, :] = right[j : j + 1]
        copies[2][x, cols : 2 + cols, :] = right[j : j + 2]


def interior_kernel(
    main_ref, left_ref, right_ref, band1_ref, band2_ref, bias1_ref, bias2_ref, out_ref, kept_ref,
    copies0, copies1, copies2, hidden, shift1, shift2, stage,
):
    rows, cols = main_ref.shape[0], main_ref.shape[1]
    channels = bias1_ref.shape[1]
    copies = (copies0, copies1, copies2)
    fill(copies, 0, main_ref[...], left_ref[...], right_ref[...])
    inner = rows - 2

    def put(half, value):
        lanes = slice(half * 2 * channels, (half + 1) * 2 * channels)
        hidden[:, :, lanes] = value
        kept_ref[0:2, :, lanes] = value[0:2]
        kept_ref[2:4, :, lanes] = value[inner - 2 :]

    first_layer(copies, band1_ref, bias1_ref, 1, inner, cols, put)
    shift1[...] = hidden[:, 1 : 1 + cols, :]
    shift2[...] = hidden[:, 2 : 2 + cols, :]
    second_layer((hidden.at[:, 0:cols, :], shift1, shift2), band2_ref, bias2_ref, 1, rows - 4, stage)
    out_ref[...] = stage[...].astype(jnp.bfloat16)


def border_kernel(
    main_ref, low_ref, high_ref, left_ref, right_ref,
    band1_ref, band2_ref, bias1_ref, bias2_ref, inner_ref, kept_ref, out_ref,
    copies0, copies1, copies2, hidden, shift1, shift2, stage,
):
    channels = bias1_ref.shape[1]
    rows, cols = main_ref.shape[0], main_ref.shape[1]
    copies = (copies0, copies1, copies2)
    left, right = left_ref[...], right_ref[...]
    for x0, ref in ((0, low_ref), (6, high_ref)):
        for x in range(2):
            corner = ref[x, cols : cols + 4, :]
            fill(copies, x0 + x, ref[x : x + 1, 0:cols, :], corner[0:2], corner[2:4])
    fill(copies, 2, main_ref[0:2], left[0:4], right[0:4])
    fill(copies, 4, main_ref[rows - 2 :], left[2 * rows - 4 :], right[2 * rows - 4 :])

    def put(half, value):
        lanes = slice(half * 2 * channels, (half + 1) * 2 * channels)
        hidden[0:2, :, lanes] = value[0:2]
        hidden[6:8, :, lanes] = value[2:4]

    first_layer(copies, band1_ref, bias1_ref, 2, 2, cols, put)
    hidden[2:6, :, :] = kept_ref[...]
    shift1[...] = hidden[:, 1 : 1 + cols, :]
    shift2[...] = hidden[:, 2 : 2 + cols, :]
    second_layer((hidden.at[:, 0:cols, :], shift1, shift2), band2_ref, bias2_ref, 2, 2, stage)
    value = stage[...].astype(jnp.bfloat16)
    border = value.shape[0] // 2
    out_ref[:border, :] = value[:border]
    out_ref[border : border + inner_ref.shape[0], :] = inner_ref[...]
    out_ref[border + inner_ref.shape[0] :, :] = value[border:]


def shards(features, pair_weight, target_tile, target_block, conv1_weight, conv1_bias, conv2_weight, conv2_bias):
    images, size, channels = features.shape[1:]
    top = target_tile.shape[2]
    n_frames = lax.axis_size("frames")
    n_rows = lax.axis_size("rows")
    devices = n_frames * n_rows
    capacity = max(2, 2 * images * top // devices)
    blocks = TX * TY * DEPTH // size
    n_c = CORES if n_rows % CORES == 0 else 1
    n_x = n_rows // n_c
    n_y = n_x if n_frames % n_x == 0 else 1
    n_z = n_frames // n_y
    shape = (n_z, n_y, n_x, n_c)
    groups = n_y * n_x
    slots = n_c * capacity
    per_group = n_z * slots
    stride = per_group + 1
    quarter = size // 4
    spans = [(part * quarter, quarter) for part in ORDER]

    def moved_by(value, dz=0, dy=0, dx=0, dc=0):
        pairs = []
        for source in range(devices):
            f, r = divmod(source, n_rows)
            z, y = divmod(f, n_y)
            x, c = divmod(r, n_c)
            z, y, x = step_to(z, dz, n_z), step_to(y, dy, n_y), step_to(x, dx, n_x)
            c = step_to(c, dc, n_c)
            pairs.append((source, ((z * n_y + y) * n_x + x) * n_c + c))
        return lax.ppermute(value, ("frames", "rows"), pairs)

    code = (target_tile * blocks + target_block).reshape(-1)
    weights = pair_weight[0].reshape(images * top, size, size)
    shared = [(weights, features[0], code)]
    for dc in range(1, n_c):
        shared.append(tuple(moved_by(v, dc=dc) for v in shared[0]))
    index, labels, own_weights, own_features = pl.pallas_call(
        functools.partial(index_kernel, shape, slots, blocks),
        out_shape=(
            jax.ShapeDtypeStruct((n_c * images * top,), jnp.int32),
            jax.ShapeDtypeStruct((groups * LABEL_ROWS, channels), jnp.bfloat16),
            jax.ShapeDtypeStruct(weights.shape, weights.dtype),
            jax.ShapeDtypeStruct(features.shape[1:], features.dtype),
        ),
        in_specs=[smem()] * n_c + [anywhere()] * 2,
        out_specs=(smem(), vmem(), anywhere(), anywhere()),
        scratch_shapes=[
            pltpu.SMEM((devices,), jnp.int32),
            pltpu.SMEM((groups * per_group + 1,), jnp.int32),
            pltpu.SemaphoreType.DMA((2,)),
        ],
        compiler_params=params(),
        name="index",
    )(*[v[2] for v in shared], weights, features[0])
    shared[0] = (own_weights, own_features, code)

    def contribute(ks):
        own = [spans[k] for k in ks]
        first = ks[0] == 0
        outs, scratch = [], []
        for _, chunk in own:
            outs += arrays(groups, per_group * chunk + (LABEL_ROWS if first else 0), channels)
            scratch.append(VMEM(((groups * per_group + 1) * chunk, channels), jnp.bfloat16))
        rows = sum(chunk for _, chunk in own)
        scratch += [
            VMEM((n_c * images * top, rows, size), jnp.bfloat16),
            pltpu.SemaphoreType.DMA((n_c,)),
            pltpu.SemaphoreType.DMA((len(outs) + groups,)),
        ]
        made = pl.pallas_call(
            functools.partial(contribute_kernel, n_c, groups, per_group, top, own, first),
            out_shape=tuple(outs),
            in_specs=[smem()] + [anywhere()] * n_c + [vmem()] * (n_c + 1),
            out_specs=(anywhere(),) * len(outs),
            scratch_shapes=scratch,
            compiler_params=params(),
        )(index, *[v[0] for v in shared], *[v[1] for v in shared], labels)
        for i, k in enumerate(ks):
            messages[k] = made[i * groups : (i + 1) * groups]

    def exchange(k):
        return [
            moved_by(value, dy=g // n_x, dx=g % n_x) if g else value
            for g, value in enumerate(messages[k])
        ]

    def merge(k, received, plan):
        first = k == 0
        chunk = spans[k][1]
        outs = arrays(n_z, blocks * chunk, channels)
        out_specs = [vmem()] * n_z
        scratch = [VMEM((n_z * blocks * chunk, channels), jnp.float32)]
        in_specs = [vmem()] * groups
        args = tuple(received)
        if first:
            outs.append(jax.ShapeDtypeStruct((stride * groups,), jnp.int32))
            out_specs.append(smem())
            scratch += [
                VMEM((groups, channels), jnp.int32),
                pltpu.SMEM((groups, channels), jnp.int32),
                pltpu.SemaphoreType.DMA,
            ]
        else:
            in_specs.append(smem())
            args += (plan,)
        return pl.pallas_call(
            functools.partial(merge_kernel, n_z, groups, slots, chunk, blocks, first),
            out_shape=tuple(outs),
            in_specs=in_specs,
            out_specs=tuple(out_specs),
            scratch_shapes=scratch,
            compiler_params=params(),
        )(*args)

    messages = {}
    contribute([0])
    contribute(list(range(1, len(spans))))
    plan, final = None, []
    for k in range(len(spans)):
        merged = merge(k, exchange(k), plan)
        if k == 0:
            plan = merged[-1]
        final += [moved_by(part, dz=dz) if dz else part for dz, part in enumerate(merged[:n_z])]
    bands = jax.ShapeDtypeStruct((3, 2, 9 * channels, 2 * channels), jnp.bfloat16)
    band1, band2 = pl.pallas_call(
        band_kernel,
        out_shape=(bands, bands),
        in_specs=[vmem(), vmem(), anywhere()],
        out_specs=(vmem(), vmem()),
        compiler_params=params(),
        name="bands",
    )(conv1_weight, conv2_weight, merged[0])
    cells = TX * TY
    lanes = DEPTH * channels
    halves = blocks // TX
    side = jax.ShapeDtypeStruct((2 * TX, lanes), jnp.bfloat16)
    left_cols, right_cols = pl.pallas_call(
        functools.partial(tail_kernel, n_z, blocks, halves),
        out_shape=(side, side),
        in_specs=[vmem()] * (2 * n_z) + [anywhere()],
        out_specs=(vmem(),) * 2,
        scratch_shapes=[VMEM((2, 2 * TX * DEPTH, channels), jnp.float32)],
        compiler_params=params(),
        name="tail",
    )(*final[: 2 * n_z], final[(len(spans) - 1) * n_z])

    def moved(value, axis, count, step):
        pairs = [(i, i + step) for i in range(count) if 0 <= i + step < count]
        return lax.ppermute(value, axis, pairs)

    left = moved(right_cols, "rows", n_rows, 1)
    right = moved(left_cols, "rows", n_rows, -1)
    wide = 80
    packed = jax.ShapeDtypeStruct((2, wide, lanes), jnp.bfloat16)
    main, first_rows, last_rows = pl.pallas_call(
        functools.partial(finish_kernel, n_z, spans, blocks, size),
        out_shape=(jax.ShapeDtypeStruct((cells, lanes), jnp.bfloat16), packed, packed),
        in_specs=[vmem()] * (len(final) + 2) + [anywhere()],
        out_specs=(vmem(),) * 3,
        scratch_shapes=[VMEM((cells * DEPTH, channels), jnp.float32)],
        compiler_params=params(),
        name="finish",
    )(*final, left, right, band1)
    low = moved(last_rows, "frames", n_frames, 1)
    high = moved(first_rows, "frames", n_frames, -1)
    main = main.reshape(TX, TY, lanes)
    bias = (conv1_bias[None], conv2_bias[None])

    def conv_scratch(height, hidden, out):
        return (
            [VMEM((height, wide, lanes), jnp.bfloat16)] * 3
            + [VMEM((hidden, wide, lanes), jnp.bfloat16)]
            + [VMEM((hidden, TY, lanes), jnp.bfloat16)] * 2
            + [VMEM((out * TY * DEPTH, channels), jnp.float32)]
        )

    inner, kept = pl.pallas_call(
        interior_kernel,
        out_shape=(
            jax.ShapeDtypeStruct(((TX - 4) * TY * DEPTH, channels), jnp.bfloat16),
            jax.ShapeDtypeStruct((4, wide, lanes), jnp.bfloat16),
        ),
        in_specs=[vmem()] * 7,
        out_specs=(vmem(),) * 2,
        scratch_shapes=conv_scratch(TX, TX - 2, TX - 4),
        compiler_params=params(),
        name="interior",
    )(main, left, right, band1, band2, *bias)
    out = pl.pallas_call(
        border_kernel,
        out_shape=jax.ShapeDtypeStruct((cells * DEPTH, channels), jnp.bfloat16),
        in_specs=[vmem()] * 11,
        out_specs=vmem(),
        scratch_shapes=conv_scratch(8, 8, 4),
        compiler_params=params(),
        name="border",
    )(main, low, high, left, right, band1, band2, *bias, inner, kept)
    return out.reshape(TX, TY, DEPTH, channels)


def solution(mesh):
    placed = (
        P("frames", "rows", None, None),
        P("frames", "rows", None, None, None),
        P("frames", "rows", None),
        P("frames", "rows", None),
        P(),
        P(),
        P(),
        P(),
    )
    return jax.shard_map(
        shards,
        mesh=mesh,
        in_specs=placed,
        out_specs=P("frames", "rows", None, None),
        check_vma=False,
    )
```

```python
import functools

import jax
import jax.numpy as jnp
from jax import lax
from jax.experimental import pallas as pl
from jax.experimental.pallas import tpu as pltpu
from jax.sharding import PartitionSpec as P


DEPTH = 4
TX = 8
TY = 64
CORES = 2
ORDER = (0, 3, 1, 2)
LABEL_ROWS = 16
VMEM = pltpu.VMEM
LIMIT = 12 * 1024 * 1024


def vmem():
    return pl.BlockSpec(memory_space=pltpu.VMEM)


def smem():
    return pl.BlockSpec(memory_space=pltpu.SMEM)


def anywhere():
    return pl.BlockSpec(memory_space=pl.ANY)


def params():
    return pltpu.CompilerParams(vmem_limit_bytes=LIMIT)


def arrays(count, rows, channels, dtype=jnp.bfloat16):
    return [jax.ShapeDtypeStruct((rows, channels), dtype)] * count


def split_low(value, count):
    if count & (count - 1) == 0:
        return value >> (count.bit_length() - 1), value & (count - 1)
    return value // count, value % count


def apart(target, source, count):
    if count & (count - 1) == 0:
        return target ^ source
    return (target - source + count) % count


def step_to(source, step, count):
    if count & (count - 1) == 0:
        return source ^ step
    return (source + step) % count


def index_kernel(shape, slots, blocks, *refs):
    n_z, n_y, n_x, n_c = shape
    codes = refs[:n_c]
    index_ref, label_ref, counts, labels = refs[n_c:]
    tiles = n_z * n_y * n_x * n_c
    groups = n_y * n_x
    spare = groups * n_z * slots

    def clear(t, carry):
        counts[t] = 0
        return carry

    lax.fori_loop(0, tiles, clear, 0, unroll=8)

    def blank(s, carry):
        labels[s] = -1
        return carry

    lax.fori_loop(0, spare, blank, 0, unroll=8)
    z, y = split_low(lax.axis_index("frames"), n_y)
    x, c = split_low(lax.axis_index("rows"), n_c)
    pairs = codes[0].shape[0]
    for source in range(n_c):
        ref = codes[source]

        def place(p, carry):
            tile, block = split_low(ref[p], blocks)
            rank = counts[tile]
            counts[tile] = rank + 1
            rest, c_to = split_low(tile, n_c)
            rest, x_to = split_low(rest, n_x)
            z_to, y_to = split_low(rest, n_y)
            group = apart(y_to, y, n_y) * n_x + apart(x_to, x, n_x)
            slot = (group * n_z + apart(z_to, z, n_z)) * slots + rank
            slot = jnp.where(c_to == c, slot, spare)
            index_ref[source * pairs + p] = slot
            labels[slot] = block
            return carry

        lax.fori_loop(0, pairs, place, 0, unroll=4)
    lane = lax.broadcasted_iota(jnp.int32, (LABEL_ROWS, label_ref.shape[1]), 1)
    for g in range(groups):
        row = jnp.full(lane.shape, -1, jnp.int32)
        for k in range(n_z * slots):
            row = jnp.where(lane == k, labels[g * n_z * slots + k], row)
        label_ref[g * LABEL_ROWS : (g + 1) * LABEL_ROWS, :] = row.astype(jnp.float32).astype(jnp.bfloat16)


def contribute_kernel(n_c, groups, per_group, images, top, spans, first, *refs):
    index_ref = refs[0]
    heads = refs[1 : 1 + n_c]
    refs = refs[1 + n_c :]
    begin, rows = min(span[0] for span in spans), sum(span[1] for span in spans)
    pairs = images * top
    size = heads[0].shape[1]
    if first:
        label_ref, refs = refs[0], refs[1:]
    else:
        sources, refs = refs[:n_c], refs[n_c:]
    outs = refs[: groups * len(spans)]
    refs = refs[groups * len(spans) :]
    buffers, refs = refs[: len(spans)], refs[len(spans) :]
    store_sems = refs[0]
    if not first:
        held, load_sems = refs[1:]
        loads = [
            pltpu.make_async_copy(
                sources[s].at[:, pl.ds(begin, rows), :], held.at[pl.ds(s * pairs, pairs)], load_sems.at[s]
            )
            for s in range(n_c)
        ]
        for load in loads:
            load.start()
    for s in range(n_c):
        if not first:
            loads[s].wait()
        base = heads[s].shape[0] - images * size

        def image(b, carry):
            p0 = s * pairs + b * top
            if first:
                weights = heads[s][pl.ds(pl.multiple_of(b * top * rows, top * rows), top * rows), :]
            else:
                weights = held[pl.ds(p0, top)].reshape(top * rows, size)
            pixels = heads[s][pl.ds(pl.multiple_of(base + b * size, size), size), :]
            product = jnp.dot(weights, pixels, preferred_element_type=jnp.float32)
            product = product.astype(jnp.bfloat16)
            for t in range(top):
                slot = index_ref[p0 + t]
                for (start, chunk), buffer in zip(spans, buffers):
                    at = t * rows + start - begin
                    buffer[pl.ds(pl.multiple_of(slot * chunk, chunk), chunk), :] = product[at : at + chunk]
            return carry

        lax.fori_loop(0, images, image, 0, unroll=4)
    copies = []
    for i, ((_, chunk), buffer) in enumerate(zip(spans, buffers)):
        length = per_group * chunk
        for g in range(groups):
            n = i * groups + g
            data = outs[n].at[pl.ds(0, length)] if first else outs[n]
            copies.append(pltpu.make_async_copy(buffer.at[pl.ds(g * length, length)], data, store_sems.at[n]))
            if first:
                copies.append(
                    pltpu.make_async_copy(
                        label_ref.at[pl.ds(g * LABEL_ROWS, LABEL_ROWS)],
                        outs[n].at[pl.ds(length, LABEL_ROWS)],
                        store_sems.at[groups * len(spans) + g],
                    )
                )
    for copy in copies:
        copy.start()
    for copy in copies:
        copy.wait()


def merge_kernel(n_z, groups, slots, chunk, blocks, first, *refs):
    messages = refs[:groups]
    refs = refs[groups:]
    per_group = n_z * slots
    stride = per_group + 1
    if first:
        outs = refs[:n_z]
        plan_ref, total, marks, marks_smem, sem = refs[n_z:]
        for g in range(groups):
            row = messages[g][per_group * chunk :, :].astype(jnp.float32)
            marks[g : g + 1, :] = row[0:1, :].astype(jnp.int32)
        copy = pltpu.make_async_copy(marks, marks_smem, sem)
        copy.start()
    else:
        plan_ref = refs[0]
        outs = refs[1 : 1 + n_z]
        (total,) = refs[1 + n_z :]
    total[...] = jnp.zeros_like(total)
    if first:
        copy.wait()
        for g in range(groups):

            def note(s, count):
                label = marks_smem[g, s]
                plan_ref[g * stride + 1 + count] = s * blocks + jnp.maximum(label, 0)
                return count + (label >= 0).astype(jnp.int32)

            plan_ref[g * stride] = lax.fori_loop(0, per_group, note, 0, unroll=8)
    for g in range(groups):

        def add(n, carry):
            slot, label = split_low(plan_ref[g * stride + 1 + n], blocks)
            step = split_low(slot, slots)[0]
            source = pl.ds(pl.multiple_of(slot * chunk, chunk), chunk)
            target = pl.ds(pl.multiple_of((step * blocks + label) * chunk, chunk), chunk)
            total[target, :] += messages[g][source, :].astype(jnp.float32)
            return carry

        lax.fori_loop(0, plan_ref[g * stride], add, 0)
    rows = blocks * chunk
    for step, out in enumerate(outs):
        out[...] = total[step * rows : (step + 1) * rows, :].astype(jnp.bfloat16)


def sum_parts(parts, block, chunk):
    value = None
    for ref in parts:
        part = ref[block * chunk : (block + 1) * chunk, :].astype(jnp.float32)
        value = part if value is None else value + part
    return value


def tail_kernel(n_z, blocks, halves, *refs):
    parts = refs[: 2 * n_z]
    left_ref, right_ref, columns = refs[2 * n_z + 1 :]
    chunk = parts[0].shape[0] // blocks
    width = 2 * DEPTH
    channels = columns.shape[2]
    for x in range(blocks // halves):
        value = sum_parts(parts[:n_z], x * halves, chunk)
        columns[0, x * width : (x + 1) * width, :] = value[:width]
        value = sum_parts(parts[n_z:], x * halves + halves - 1, chunk)
        columns[1, x * width : (x + 1) * width, :] = value[chunk - width :]
    cells = columns.shape[1] // DEPTH
    for side, ref in enumerate((left_ref, right_ref)):
        for z in range(DEPTH):
            part = columns[side, pl.ds(z, cells, stride=DEPTH), :].astype(jnp.bfloat16)
            ref[:, z * channels : (z + 1) * channels] = part


def finish_kernel(n_z, spans, blocks, size, *refs):
    count = n_z * len(spans)
    parts = refs[:count]
    left_ref, right_ref, _, out_ref, first_ref, last_ref, total = refs[count:]
    for k, (start, chunk) in enumerate(spans):
        for block in range(blocks):
            at = block * size + start
            total[at : at + chunk, :] = sum_parts(parts[k * n_z : (k + 1) * n_z], block, chunk)
    cells = total.shape[0] // DEPTH
    channels = total.shape[1]
    for z in range(DEPTH):
        part = total[pl.ds(z, cells, stride=DEPTH), :].astype(jnp.bfloat16)
        lanes = slice(z * channels, (z + 1) * channels)
        out_ref[:, lanes] = part
        for x in range(2):
            first_ref[x, 0:TY, lanes] = part[x * TY : (x + 1) * TY]
            last_ref[x, 0:TY, lanes] = part[cells - (2 - x) * TY : cells - (1 - x) * TY]
    rows = cells // TY
    for x in range(2):
        for ref, at in ((first_ref, x), (last_ref, rows - 2 + x)):
            ref[x, TY : TY + 2, :] = left_ref[2 * at : 2 * at + 2, :]
            ref[x, TY + 2 : TY + 4, :] = right_ref[2 * at : 2 * at + 2, :]


def band_kernel(first_ref, second_ref, after_ref, out1_ref, out2_ref):
    channels = first_ref.shape[-1]
    zero = jnp.zeros((channels, channels), jnp.bfloat16)
    for source, target in ((first_ref, out1_ref), (second_ref, out2_ref)):
        for dx in range(3):
            for half in range(2):
                for dy in range(3):
                    for k in range(3):
                        z_in = k + half
                        for j in range(2):
                            dz = z_in - (2 * half + j) + 1
                            value = source[dx, dy, dz] if 0 <= dz < 3 else zero
                            row = (dy * 3 + k) * channels
                            target[dx, half, row : row + channels, j * channels : (j + 1) * channels] = value


def silu(v):
    return v / (1.0 + jnp.exp(-v))


def convolve_half(copies, bands, half, slabs, out_rows, channels):
    total = None
    for dx in range(3):
        pieces = []
        for dy in range(3):
            lanes = slice(half * channels, (half + 3) * channels)
            height = copies[dy].shape[0] // slabs
            parts = [copies[dy][s * height + dx : s * height + dx + out_rows, :, lanes] for s in range(slabs)]
            piece = parts[0] if slabs == 1 else jnp.concatenate(parts, axis=0)
            pieces.append(piece.reshape(-1, 3 * channels))
        product = jnp.dot(
            jnp.concatenate(pieces, axis=1), bands[dx, half], preferred_element_type=jnp.float32
        )
        total = product if total is None else total + product
    return total


def volume_ends():
    ends = []
    for axis in ("frames", "rows"):
        at = lax.axis_index(axis)
        ends += [(at == 0).astype(jnp.int32), (at == lax.axis_size(axis) - 1).astype(jnp.int32)]
    return ends


def first_layer(copies, band_ref, bias_ref, slabs, out_rows, cols, put):
    ends = volume_ends()
    channels = bias_ref.shape[1]
    bias = jnp.concatenate([bias_ref[...], bias_ref[...]], axis=1)
    for half in range(2):
        total = convolve_half(copies, band_ref, half, slabs, out_rows, channels)
        value = silu(total + bias).reshape(slabs * out_rows, -1, 2 * channels)
        y_at = lax.broadcasted_iota(jnp.int32, value.shape, 1)
        keep = (y_at >= ends[2]) & (y_at < cols + 2 - ends[3])
        if slabs > 1:
            x_at = lax.broadcasted_iota(jnp.int32, value.shape, 0)
            keep = keep & (x_at >= ends[0]) & (x_at < slabs * out_rows - ends[1])
        value = jnp.where(keep, value, 0.0).astype(jnp.bfloat16)
        put(half, value)


def second_layer(copies, band_ref, bias_ref, slabs, out_rows, stage):
    channels = bias_ref.shape[1]
    cells = stage.shape[0] // DEPTH
    for half in range(2):
        total = convolve_half(copies, band_ref, half, slabs, out_rows, channels)
        for j in range(2):
            value = silu(total[:, j * channels : (j + 1) * channels] + bias_ref[...])
            stage[pl.ds(2 * half + j, cells, stride=DEPTH), :] = value


def fill(copies, x0, value, left, right):
    cols = value.shape[1]
    part = slice(x0, x0 + value.shape[0])
    copies[0][part, 2 : 2 + cols, :] = value
    copies[1][part, 1 : 1 + cols, :] = value
    copies[2][part, 0:cols, :] = value
    for i in range(value.shape[0]):
        x, j = x0 + i, 2 * i
        copies[0][x, 0:2, :] = left[j : j + 2]
        copies[1][x, 0:1, :] = left[j + 1 : j + 2]
        copies[1][x, 1 + cols : 2 + cols, :] = right[j : j + 1]
        copies[2][x, cols : 2 + cols, :] = right[j : j + 2]


def interior_kernel(
    main_ref, left_ref, right_ref, band1_ref, band2_ref, bias1_ref, bias2_ref, out_ref, kept_ref,
    copies0, copies1, copies2, hidden, shift1, shift2, stage,
):
    rows, cols = main_ref.shape[0], main_ref.shape[1]
    channels = bias1_ref.shape[1]
    copies = (copies0, copies1, copies2)
    fill(copies, 0, main_ref[...], left_ref[...], right_ref[...])
    inner = rows - 2

    def put(half, value):
        lanes = slice(half * 2 * channels, (half + 1) * 2 * channels)
        hidden[:, :, lanes] = value
        kept_ref[0:2, :, lanes] = value[0:2]
        kept_ref[2:4, :, lanes] = value[inner - 2 :]

    first_layer(copies, band1_ref, bias1_ref, 1, inner, cols, put)
    shift1[...] = hidden[:, 1 : 1 + cols, :]
    shift2[...] = hidden[:, 2 : 2 + cols, :]
    second_layer((hidden.at[:, 0:cols, :], shift1, shift2), band2_ref, bias2_ref, 1, rows - 4, stage)
    out_ref[...] = stage[...].astype(jnp.bfloat16)


def border_kernel(
    main_ref, low_ref, high_ref, left_ref, right_ref,
    band1_ref, band2_ref, bias1_ref, bias2_ref, inner_ref, kept_ref, out_ref,
    copies0, copies1, copies2, hidden, shift1, shift2, stage,
):
    channels = bias1_ref.shape[1]
    rows, cols = main_ref.shape[0], main_ref.shape[1]
    copies = (copies0, copies1, copies2)
    left, right = left_ref[...], right_ref[...]
    for x0, ref in ((0, low_ref), (6, high_ref)):
        for x in range(2):
            corner = ref[x, cols : cols + 4, :]
            fill(copies, x0 + x, ref[x : x + 1, 0:cols, :], corner[0:2], corner[2:4])
    fill(copies, 2, main_ref[0:2], left[0:4], right[0:4])
    fill(copies, 4, main_ref[rows - 2 :], left[2 * rows - 4 :], right[2 * rows - 4 :])

    def put(half, value):
        lanes = slice(half * 2 * channels, (half + 1) * 2 * channels)
        hidden[0:2, :, lanes] = value[0:2]
        hidden[6:8, :, lanes] = value[2:4]

    first_layer(copies, band1_ref, bias1_ref, 2, 2, cols, put)
    hidden[2:6, :, :] = kept_ref[...]
    shift1[...] = hidden[:, 1 : 1 + cols, :]
    shift2[...] = hidden[:, 2 : 2 + cols, :]
    second_layer((hidden.at[:, 0:cols, :], shift1, shift2), band2_ref, bias2_ref, 2, 2, stage)
    value = stage[...].astype(jnp.bfloat16)
    border = value.shape[0] // 2
    out_ref[:border, :] = value[:border]
    out_ref[border : border + inner_ref.shape[0], :] = inner_ref[...]
    out_ref[border + inner_ref.shape[0] :, :] = value[border:]


def shards(features, pair_weight, target_tile, target_block, conv1_weight, conv1_bias, conv2_weight, conv2_bias):
    images, size, channels = features.shape[1:]
    top = target_tile.shape[2]
    n_frames = lax.axis_size("frames")
    n_rows = lax.axis_size("rows")
    devices = n_frames * n_rows
    capacity = max(2, 2 * images * top // devices)
    blocks = TX * TY * DEPTH // size
    n_c = CORES if n_rows % CORES == 0 else 1
    n_x = n_rows // n_c
    n_y = n_x if n_frames % n_x == 0 else 1
    n_z = n_frames // n_y
    shape = (n_z, n_y, n_x, n_c)
    groups = n_y * n_x
    slots = n_c * capacity
    per_group = n_z * slots
    stride = per_group + 1
    quarter = size // 4
    spans = [(part * quarter, quarter) for part in ORDER]

    def moved_by(value, dz=0, dy=0, dx=0, dc=0):
        pairs = []
        for source in range(devices):
            f, r = divmod(source, n_rows)
            z, y = divmod(f, n_y)
            x, c = divmod(r, n_c)
            z, y, x = step_to(z, dz, n_z), step_to(y, dy, n_y), step_to(x, dx, n_x)
            c = step_to(c, dc, n_c)
            pairs.append((source, ((z * n_y + y) * n_x + x) * n_c + c))
        return lax.ppermute(value, ("frames", "rows"), pairs)

    code = (target_tile * blocks + target_block).reshape(-1)
    weights = pair_weight[0].reshape(images * top, size, size)
    begin, rows = spans[0]
    head = jnp.concatenate(
        [weights[:, begin : begin + rows].reshape(-1, size), features[0].reshape(-1, channels)], axis=0
    )
    shared = [(code, head, weights)]
    for dc in range(1, n_c):
        shared.append(tuple(moved_by(v, dc=dc) for v in shared[0]))
    index, labels = pl.pallas_call(
        functools.partial(index_kernel, shape, slots, blocks),
        out_shape=(
            jax.ShapeDtypeStruct((n_c * images * top,), jnp.int32),
            jax.ShapeDtypeStruct((groups * LABEL_ROWS, channels), jnp.bfloat16),
        ),
        in_specs=[smem()] * n_c,
        out_specs=(smem(), vmem()),
        scratch_shapes=[pltpu.SMEM((devices,), jnp.int32), pltpu.SMEM((groups * per_group + 1,), jnp.int32)],
        compiler_params=params(),
        name="index",
    )(*[v[0] for v in shared])

    def contribute(ks):
        own = [spans[k] for k in ks]
        first = ks[0] == 0
        outs, scratch = [], []
        for _, chunk in own:
            outs += arrays(groups, per_group * chunk + (LABEL_ROWS if first else 0), channels)
            scratch.append(VMEM(((groups * per_group + 1) * chunk, channels), jnp.bfloat16))
        rows = sum(chunk for _, chunk in own)
        scratch.append(pltpu.SemaphoreType.DMA((len(outs) + groups,)))
        in_specs = [smem()] + [vmem()] * n_c
        args = [index] + [v[1] for v in shared]
        if first:
            in_specs.append(vmem())
            args.append(labels)
        else:
            in_specs += [anywhere()] * n_c
            args += [v[2] for v in shared]
            scratch += [
                VMEM((n_c * images * top, rows, size), jnp.bfloat16),
                pltpu.SemaphoreType.DMA((n_c,)),
            ]
        made = pl.pallas_call(
            functools.partial(contribute_kernel, n_c, groups, per_group, images, top, own, first),
            out_shape=tuple(outs),
            in_specs=in_specs,
            out_specs=(anywhere(),) * len(outs),
            scratch_shapes=scratch,
            compiler_params=params(),
        )(*args)
        for i, k in enumerate(ks):
            messages[k] = made[i * groups : (i + 1) * groups]

    def exchange(k):
        return [
            moved_by(value, dy=g // n_x, dx=g % n_x) if g else value
            for g, value in enumerate(messages[k])
        ]

    def merge(k, received, plan):
        first = k == 0
        chunk = spans[k][1]
        outs = arrays(n_z, blocks * chunk, channels)
        out_specs = [vmem()] * n_z
        scratch = [VMEM((n_z * blocks * chunk, channels), jnp.float32)]
        in_specs = [vmem()] * groups
        args = tuple(received)
        if first:
            outs.append(jax.ShapeDtypeStruct((stride * groups,), jnp.int32))
            out_specs.append(smem())
            scratch += [
                VMEM((groups, channels), jnp.int32),
                pltpu.SMEM((groups, channels), jnp.int32),
                pltpu.SemaphoreType.DMA,
            ]
        else:
            in_specs.append(smem())
            args += (plan,)
        return pl.pallas_call(
            functools.partial(merge_kernel, n_z, groups, slots, chunk, blocks, first),
            out_shape=tuple(outs),
            in_specs=in_specs,
            out_specs=tuple(out_specs),
            scratch_shapes=scratch,
            compiler_params=params(),
        )(*args)

    messages = {}
    contribute([0])
    contribute(list(range(1, len(spans))))
    plan, final = None, []
    for k in range(len(spans)):
        merged = merge(k, exchange(k), plan)
        if k == 0:
            plan = merged[-1]
        final += [moved_by(part, dz=dz) if dz else part for dz, part in enumerate(merged[:n_z])]
    bands = jax.ShapeDtypeStruct((3, 2, 9 * channels, 2 * channels), jnp.bfloat16)
    band1, band2 = pl.pallas_call(
        band_kernel,
        out_shape=(bands, bands),
        in_specs=[vmem(), vmem(), anywhere()],
        out_specs=(vmem(), vmem()),
        compiler_params=params(),
        name="bands",
    )(conv1_weight, conv2_weight, merged[0])
    cells = TX * TY
    lanes = DEPTH * channels
    halves = blocks // TX
    side = jax.ShapeDtypeStruct((2 * TX, lanes), jnp.bfloat16)
    left_cols, right_cols = pl.pallas_call(
        functools.partial(tail_kernel, n_z, blocks, halves),
        out_shape=(side, side),
        in_specs=[vmem()] * (2 * n_z) + [anywhere()],
        out_specs=(vmem(),) * 2,
        scratch_shapes=[VMEM((2, 2 * TX * DEPTH, channels), jnp.float32)],
        compiler_params=params(),
        name="tail",
    )(*final[: 2 * n_z], final[(len(spans) - 1) * n_z])

    def moved(value, axis, count, step):
        pairs = [(i, i + step) for i in range(count) if 0 <= i + step < count]
        return lax.ppermute(value, axis, pairs)

    left = moved(right_cols, "rows", n_rows, 1)
    right = moved(left_cols, "rows", n_rows, -1)
    wide = 80
    packed = jax.ShapeDtypeStruct((2, wide, lanes), jnp.bfloat16)
    main, first_rows, last_rows = pl.pallas_call(
        functools.partial(finish_kernel, n_z, spans, blocks, size),
        out_shape=(jax.ShapeDtypeStruct((cells, lanes), jnp.bfloat16), packed, packed),
        in_specs=[vmem()] * (len(final) + 2) + [anywhere()],
        out_specs=(vmem(),) * 3,
        scratch_shapes=[VMEM((cells * DEPTH, channels), jnp.float32)],
        compiler_params=params(),
        name="finish",
    )(*final, left, right, band1)
    low = moved(last_rows, "frames", n_frames, 1)
    high = moved(first_rows, "frames", n_frames, -1)
    main = main.reshape(TX, TY, lanes)
    bias = (conv1_bias[None], conv2_bias[None])

    def conv_scratch(height, hidden, out):
        return (
            [VMEM((height, wide, lanes), jnp.bfloat16)] * 3
            + [VMEM((hidden, wide, lanes), jnp.bfloat16)]
            + [VMEM((hidden, TY, lanes), jnp.bfloat16)] * 2
            + [VMEM((out * TY * DEPTH, channels), jnp.float32)]
        )

    inner, kept = pl.pallas_call(
        interior_kernel,
        out_shape=(
            jax.ShapeDtypeStruct(((TX - 4) * TY * DEPTH, channels), jnp.bfloat16),
            jax.ShapeDtypeStruct((4, wide, lanes), jnp.bfloat16),
        ),
        in_specs=[vmem()] * 7,
        out_specs=(vmem(),) * 2,
        scratch_shapes=conv_scratch(TX, TX - 2, TX - 4),
        compiler_params=params(),
        name="interior",
    )(main, left, right, band1, band2, *bias)
    out = pl.pallas_call(
        border_kernel,
        out_shape=jax.ShapeDtypeStruct((cells * DEPTH, channels), jnp.bfloat16),
        in_specs=[vmem()] * 11,
        out_specs=vmem(),
        scratch_shapes=conv_scratch(8, 8, 4),
        compiler_params=params(),
        name="border",
    )(main, low, high, left, right, band1, band2, *bias, inner, kept)
    return out.reshape(TX, TY, DEPTH, channels)


def solution(mesh):
    placed = (
        P("frames", "rows", None, None),
        P("frames", "rows", None, None, None),
        P("frames", "rows", None),
        P("frames", "rows", None),
        P(),
        P(),
        P(),
        P(),
    )
    return jax.shard_map(
        shards,
        mesh=mesh,
        in_specs=placed,
        out_specs=P("frames", "rows", None, None),
        check_vma=False,
    )
```

```python
import functools

import jax
import jax.numpy as jnp
from jax import lax
from jax.experimental import pallas as pl
from jax.experimental.pallas import tpu as pltpu
from jax.sharding import PartitionSpec as P


DEPTH = 4
TX = 8
TY = 64
CORES = 2
ORDER = (0, 3, 1, 2)
LABEL_ROWS = 16
VMEM = pltpu.VMEM
LIMIT = 12 * 1024 * 1024


def vmem():
    return pl.BlockSpec(memory_space=pltpu.VMEM)


def smem():
    return pl.BlockSpec(memory_space=pltpu.SMEM)


def anywhere():
    return pl.BlockSpec(memory_space=pl.ANY)


def params():
    return pltpu.CompilerParams(vmem_limit_bytes=LIMIT)


def arrays(count, rows, channels, dtype=jnp.bfloat16):
    return [jax.ShapeDtypeStruct((rows, channels), dtype)] * count


def split_low(value, count):
    if count & (count - 1) == 0:
        return value >> (count.bit_length() - 1), value & (count - 1)
    return value // count, value % count


def apart(target, source, count):
    if count & (count - 1) == 0:
        return target ^ source
    return (target - source + count) % count


def step_to(source, step, count):
    if count & (count - 1) == 0:
        return source ^ step
    return (source + step) % count


def index_kernel(shape, slots, blocks, *refs):
    n_z, n_y, n_x, n_c = shape
    codes = refs[:n_c]
    index_ref, label_ref, label2_ref, counts, labels, labels2 = refs[n_c:]
    tiles = n_z * n_y * n_x * n_c
    groups = n_y * n_x
    spare = groups * n_z * slots

    def clear(t, carry):
        counts[t] = 0
        return carry

    lax.fori_loop(0, tiles, clear, 0, unroll=8)

    def blank(s, carry):
        labels[s] = -1
        labels2[s] = -1
        return carry

    lax.fori_loop(0, spare, blank, 0, unroll=8)
    z, y = split_low(lax.axis_index("frames"), n_y)
    x, c = split_low(lax.axis_index("rows"), n_c)
    pairs = codes[0].shape[0]
    for source in range(n_c):
        ref = codes[source]

        def place(p, carry):
            tile, block = split_low(ref[p], blocks)
            rank = counts[tile]
            counts[tile] = rank + 1
            rest, c_to = split_low(tile, n_c)
            rest, x_to = split_low(rest, n_x)
            z_to, y_to = split_low(rest, n_y)
            group = apart(y_to, y, n_y) * n_x + apart(x_to, x, n_x)
            step = apart(z_to, z, n_z)
            slot = jnp.where(c_to == c, (group * n_z + step) * slots + rank, spare)
            slot2 = jnp.where(c_to == c, (step * groups + group) * slots + rank, spare)
            index_ref[source * pairs + p] = slot
            index_ref[(n_c + source) * pairs + p] = slot2
            labels[slot] = block
            labels2[slot2] = block
            return carry

        lax.fori_loop(0, pairs, place, 0, unroll=4)
    lane = lax.broadcasted_iota(jnp.int32, (LABEL_ROWS, label_ref.shape[1]), 1)
    for source, target, outer in ((labels, label_ref, groups), (labels2, label2_ref, n_z)):
        inner = spare // outer
        for g in range(outer):
            row = jnp.full(lane.shape, -1, jnp.int32)
            for k in range(inner):
                row = jnp.where(lane == k, source[g * inner + k], row)
            target[g * LABEL_ROWS : (g + 1) * LABEL_ROWS, :] = row.astype(jnp.float32).astype(jnp.bfloat16)


def contribute_kernel(n_c, outer, per_group, images, top, spans, base, direct, labelled, *refs):
    index_ref = refs[0]
    heads = refs[1 : 1 + n_c]
    refs = refs[1 + n_c :]
    rows = sum(span[1] for span in spans)
    pairs = images * top
    size = heads[0].shape[1]
    if labelled:
        label_ref, refs = refs[0], refs[1:]
    if not direct:
        sources, refs = refs[:n_c], refs[n_c:]
    outs = refs[: outer * len(spans)]
    refs = refs[outer * len(spans) :]
    buffers, refs = refs[: len(spans)], refs[len(spans) :]
    store_sems = refs[0]
    if not direct:
        held, load_sems = refs[1:]
        loads = []
        for s in range(n_c):
            at = 0
            for i, (start, chunk) in enumerate(spans):
                loads.append(
                    pltpu.make_async_copy(
                        sources[s].at[:, pl.ds(start, chunk), :],
                        held.at[pl.ds(s * pairs, pairs), pl.ds(at, chunk)],
                        load_sems.at[s * len(spans) + i],
                    )
                )
                at += chunk
        for load in loads:
            load.start()
    for s in range(n_c):
        if not direct:
            for load in loads[s * len(spans) : (s + 1) * len(spans)]:
                load.wait()
        pixel_base = heads[s].shape[0] - images * size

        def image(b, carry):
            p0 = s * pairs + b * top
            if direct:
                weights = heads[s][pl.ds(pl.multiple_of(b * top * rows, top * rows), top * rows), :]
            else:
                weights = held[pl.ds(p0, top)].reshape(top * rows, size)
            pixels = heads[s][pl.ds(pl.multiple_of(pixel_base + b * size, size), size), :]
            product = jnp.dot(weights, pixels, preferred_element_type=jnp.float32)
            product = product.astype(jnp.bfloat16)
            for t in range(top):
                slot = index_ref[base + p0 + t]
                at = t * rows
                for (_, chunk), buffer in zip(spans, buffers):
                    buffer[pl.ds(pl.multiple_of(slot * chunk, chunk), chunk), :] = product[at : at + chunk]
                    at += chunk
            return carry

        lax.fori_loop(0, images, image, 0, unroll=4)
    copies = []
    for i, ((_, chunk), buffer) in enumerate(zip(spans, buffers)):
        length = per_group * chunk
        for g in range(outer):
            n = i * outer + g
            data = outs[n].at[pl.ds(0, length)] if labelled else outs[n]
            copies.append(pltpu.make_async_copy(buffer.at[pl.ds(g * length, length)], data, store_sems.at[n]))
            if labelled:
                copies.append(
                    pltpu.make_async_copy(
                        label_ref.at[pl.ds(g * LABEL_ROWS, LABEL_ROWS)],
                        outs[n].at[pl.ds(length, LABEL_ROWS)],
                        store_sems.at[outer * len(spans) + n],
                    )
                )
    for copy in copies:
        copy.start()
    for copy in copies:
        copy.wait()


def merge_kernel(n_z, groups, slots, chunk, blocks, first, *refs):
    messages = refs[:groups]
    refs = refs[groups:]
    per_group = n_z * slots
    stride = per_group + 1
    if first:
        outs = refs[:n_z]
        plan_ref, total, marks, marks_smem, sem = refs[n_z:]
        for g in range(groups):
            row = messages[g][per_group * chunk :, :].astype(jnp.float32)
            marks[g : g + 1, :] = row[0:1, :].astype(jnp.int32)
        copy = pltpu.make_async_copy(marks, marks_smem, sem)
        copy.start()
    else:
        plan_ref = refs[0]
        outs = refs[1 : 1 + n_z]
        (total,) = refs[1 + n_z :]
    total[...] = jnp.zeros_like(total)
    if first:
        copy.wait()
        for g in range(groups):

            def note(s, count):
                label = marks_smem[g, s]
                plan_ref[g * stride + 1 + count] = s * blocks + jnp.maximum(label, 0)
                return count + (label >= 0).astype(jnp.int32)

            plan_ref[g * stride] = lax.fori_loop(0, per_group, note, 0, unroll=8)
    for g in range(groups):

        def add(n, carry):
            slot, label = split_low(plan_ref[g * stride + 1 + n], blocks)
            step = split_low(slot, slots)[0]
            source = pl.ds(pl.multiple_of(slot * chunk, chunk), chunk)
            target = pl.ds(pl.multiple_of((step * blocks + label) * chunk, chunk), chunk)
            total[target, :] += messages[g][source, :].astype(jnp.float32)
            return carry

        lax.fori_loop(0, plan_ref[g * stride], add, 0)
    rows = blocks * chunk
    for step, out in enumerate(outs):
        out[...] = total[step * rows : (step + 1) * rows, :].astype(jnp.bfloat16)


def sum_parts(parts, block, chunk):
    value = None
    for ref in parts:
        part = ref[block * chunk : (block + 1) * chunk, :].astype(jnp.float32)
        value = part if value is None else value + part
    return value


def tail_kernel(n_z, blocks, halves, *refs):
    parts = refs[: 2 * n_z]
    left_ref, right_ref, columns = refs[2 * n_z + 1 :]
    chunk = parts[0].shape[0] // blocks
    width = 2 * DEPTH
    channels = columns.shape[2]
    for x in range(blocks // halves):
        value = sum_parts(parts[:n_z], x * halves, chunk)
        columns[0, x * width : (x + 1) * width, :] = value[:width]
        value = sum_parts(parts[n_z:], x * halves + halves - 1, chunk)
        columns[1, x * width : (x + 1) * width, :] = value[chunk - width :]
    cells = columns.shape[1] // DEPTH
    for side, ref in enumerate((left_ref, right_ref)):
        for z in range(DEPTH):
            part = columns[side, pl.ds(z, cells, stride=DEPTH), :].astype(jnp.bfloat16)
            ref[:, z * channels : (z + 1) * channels] = part


def finish_kernel(spans, counts, blocks, size, *refs):
    left_ref, right_ref, _, out_ref, first_ref, last_ref, total = refs[sum(counts) :]
    parts = 0
    for (start, chunk), count in zip(spans, counts):
        for block in range(blocks):
            at = block * size + start
            total[at : at + chunk, :] = sum_parts(refs[parts : parts + count], block, chunk)
        parts += count
    cells = total.shape[0] // DEPTH
    channels = total.shape[1]
    for z in range(DEPTH):
        part = total[pl.ds(z, cells, stride=DEPTH), :].astype(jnp.bfloat16)
        lanes = slice(z * channels, (z + 1) * channels)
        out_ref[:, lanes] = part
        for x in range(2):
            first_ref[x, 0:TY, lanes] = part[x * TY : (x + 1) * TY]
            last_ref[x, 0:TY, lanes] = part[cells - (2 - x) * TY : cells - (1 - x) * TY]
    rows = cells // TY
    for x in range(2):
        for ref, at in ((first_ref, x), (last_ref, rows - 2 + x)):
            ref[x, TY : TY + 2, :] = left_ref[2 * at : 2 * at + 2, :]
            ref[x, TY + 2 : TY + 4, :] = right_ref[2 * at : 2 * at + 2, :]


def band_kernel(first_ref, second_ref, after_ref, out1_ref, out2_ref):
    channels = first_ref.shape[-1]
    zero = jnp.zeros((channels, channels), jnp.bfloat16)
    for source, target in ((first_ref, out1_ref), (second_ref, out2_ref)):
        for dx in range(3):
            for half in range(2):
                for dy in range(3):
                    for k in range(3):
                        z_in = k + half
                        for j in range(2):
                            dz = z_in - (2 * half + j) + 1
                            value = source[dx, dy, dz] if 0 <= dz < 3 else zero
                            row = (dy * 3 + k) * channels
                            target[dx, half, row : row + channels, j * channels : (j + 1) * channels] = value


def silu(v):
    return v / (1.0 + jnp.exp(-v))


def convolve_half(copies, bands, half, slabs, out_rows, channels):
    total = None
    for dx in range(3):
        pieces = []
        for dy in range(3):
            lanes = slice(half * channels, (half + 3) * channels)
            height = copies[dy].shape[0] // slabs
            parts = [copies[dy][s * height + dx : s * height + dx + out_rows, :, lanes] for s in range(slabs)]
            piece = parts[0] if slabs == 1 else jnp.concatenate(parts, axis=0)
            pieces.append(piece.reshape(-1, 3 * channels))
        product = jnp.dot(
            jnp.concatenate(pieces, axis=1), bands[dx, half], preferred_element_type=jnp.float32
        )
        total = product if total is None else total + product
    return total


def volume_ends():
    ends = []
    for axis in ("frames", "rows"):
        at = lax.axis_index(axis)
        ends += [(at == 0).astype(jnp.int32), (at == lax.axis_size(axis) - 1).astype(jnp.int32)]
    return ends


def first_layer(copies, band_ref, bias_ref, slabs, out_rows, cols, put):
    ends = volume_ends()
    channels = bias_ref.shape[1]
    bias = jnp.concatenate([bias_ref[...], bias_ref[...]], axis=1)
    for half in range(2):
        total = convolve_half(copies, band_ref, half, slabs, out_rows, channels)
        value = silu(total + bias).reshape(slabs * out_rows, -1, 2 * channels)
        y_at = lax.broadcasted_iota(jnp.int32, value.shape, 1)
        keep = (y_at >= ends[2]) & (y_at < cols + 2 - ends[3])
        if slabs > 1:
            x_at = lax.broadcasted_iota(jnp.int32, value.shape, 0)
            keep = keep & (x_at >= ends[0]) & (x_at < slabs * out_rows - ends[1])
        value = jnp.where(keep, value, 0.0).astype(jnp.bfloat16)
        put(half, value)


def second_layer(copies, band_ref, bias_ref, slabs, out_rows, stage):
    channels = bias_ref.shape[1]
    cells = stage.shape[0] // DEPTH
    for half in range(2):
        total = convolve_half(copies, band_ref, half, slabs, out_rows, channels)
        for j in range(2):
            value = silu(total[:, j * channels : (j + 1) * channels] + bias_ref[...])
            stage[pl.ds(2 * half + j, cells, stride=DEPTH), :] = value


def fill(copies, x0, value, left, right):
    cols = value.shape[1]
    part = slice(x0, x0 + value.shape[0])
    copies[0][part, 2 : 2 + cols, :] = value
    copies[1][part, 1 : 1 + cols, :] = value
    copies[2][part, 0:cols, :] = value
    for i in range(value.shape[0]):
        x, j = x0 + i, 2 * i
        copies[0][x, 0:2, :] = left[j : j + 2]
        copies[1][x, 0:1, :] = left[j + 1 : j + 2]
        copies[1][x, 1 + cols : 2 + cols, :] = right[j : j + 1]
        copies[2][x, cols : 2 + cols, :] = right[j : j + 2]


def interior_kernel(
    main_ref, left_ref, right_ref, band1_ref, band2_ref, bias1_ref, bias2_ref, out_ref, kept_ref,
    copies0, copies1, copies2, hidden, shift1, shift2, stage,
):
    rows, cols = main_ref.shape[0], main_ref.shape[1]
    channels = bias1_ref.shape[1]
    copies = (copies0, copies1, copies2)
    fill(copies, 0, main_ref[...], left_ref[...], right_ref[...])
    inner = rows - 2

    def put(half, value):
        lanes = slice(half * 2 * channels, (half + 1) * 2 * channels)
        hidden[:, :, lanes] = value
        kept_ref[0:2, :, lanes] = value[0:2]
        kept_ref[2:4, :, lanes] = value[inner - 2 :]

    first_layer(copies, band1_ref, bias1_ref, 1, inner, cols, put)
    shift1[...] = hidden[:, 1 : 1 + cols, :]
    shift2[...] = hidden[:, 2 : 2 + cols, :]
    second_layer((hidden.at[:, 0:cols, :], shift1, shift2), band2_ref, bias2_ref, 1, rows - 4, stage)
    out_ref[...] = stage[...].astype(jnp.bfloat16)


def border_kernel(
    main_ref, low_ref, high_ref, left_ref, right_ref,
    band1_ref, band2_ref, bias1_ref, bias2_ref, inner_ref, kept_ref, out_ref,
    copies0, copies1, copies2, hidden, shift1, shift2, stage,
):
    channels = bias1_ref.shape[1]
    rows, cols = main_ref.shape[0], main_ref.shape[1]
    copies = (copies0, copies1, copies2)
    left, right = left_ref[...], right_ref[...]
    for x0, ref in ((0, low_ref), (6, high_ref)):
        for x in range(2):
            corner = ref[x, cols : cols + 4, :]
            fill(copies, x0 + x, ref[x : x + 1, 0:cols, :], corner[0:2], corner[2:4])
    fill(copies, 2, main_ref[0:2], left[0:4], right[0:4])
    fill(copies, 4, main_ref[rows - 2 :], left[2 * rows - 4 :], right[2 * rows - 4 :])

    def put(half, value):
        lanes = slice(half * 2 * channels, (half + 1) * 2 * channels)
        hidden[0:2, :, lanes] = value[0:2]
        hidden[6:8, :, lanes] = value[2:4]

    first_layer(copies, band1_ref, bias1_ref, 2, 2, cols, put)
    hidden[2:6, :, :] = kept_ref[...]
    shift1[...] = hidden[:, 1 : 1 + cols, :]
    shift2[...] = hidden[:, 2 : 2 + cols, :]
    second_layer((hidden.at[:, 0:cols, :], shift1, shift2), band2_ref, bias2_ref, 2, 2, stage)
    value = stage[...].astype(jnp.bfloat16)
    border = value.shape[0] // 2
    out_ref[:border, :] = value[:border]
    out_ref[border : border + inner_ref.shape[0], :] = inner_ref[...]
    out_ref[border + inner_ref.shape[0] :, :] = value[border:]


def shards(features, pair_weight, target_tile, target_block, conv1_weight, conv1_bias, conv2_weight, conv2_bias):
    images, size, channels = features.shape[1:]
    top = target_tile.shape[2]
    n_frames = lax.axis_size("frames")
    n_rows = lax.axis_size("rows")
    devices = n_frames * n_rows
    capacity = max(2, 2 * images * top // devices)
    blocks = TX * TY * DEPTH // size
    n_c = CORES if n_rows % CORES == 0 else 1
    n_x = n_rows // n_c
    n_y = n_x if n_frames % n_x == 0 else 1
    n_z = n_frames // n_y
    shape = (n_z, n_y, n_x, n_c)
    groups = n_y * n_x
    slots = n_c * capacity
    quarter = size // 4
    spans = [(part * quarter, quarter) for part in ORDER]

    def moved_by(value, dz=0, dy=0, dx=0, dc=0):
        pairs = []
        for source in range(devices):
            f, r = divmod(source, n_rows)
            z, y = divmod(f, n_y)
            x, c = divmod(r, n_c)
            z, y, x = step_to(z, dz, n_z), step_to(y, dy, n_y), step_to(x, dx, n_x)
            c = step_to(c, dc, n_c)
            pairs.append((source, ((z * n_y + y) * n_x + x) * n_c + c))
        return lax.ppermute(value, ("frames", "rows"), pairs)

    code = (target_tile * blocks + target_block).reshape(-1)
    weights = pair_weight[0].reshape(images * top, size, size)
    turned = len(spans) - 1
    begin, rows = spans[turned]
    head = jnp.concatenate(
        [weights[:, begin : begin + rows].reshape(-1, size), features[0].reshape(-1, channels)], axis=0
    )
    shared = [(code, head, weights)]
    for dc in range(1, n_c):
        shared.append(tuple(moved_by(v, dc=dc) for v in shared[0]))
    index, labels, labels_turned = pl.pallas_call(
        functools.partial(index_kernel, shape, slots, blocks),
        out_shape=(
            jax.ShapeDtypeStruct((2 * n_c * images * top,), jnp.int32),
            jax.ShapeDtypeStruct((groups * LABEL_ROWS, channels), jnp.bfloat16),
            jax.ShapeDtypeStruct((n_z * LABEL_ROWS, channels), jnp.bfloat16),
        ),
        in_specs=[smem()] * n_c,
        out_specs=(smem(), vmem(), vmem()),
        scratch_shapes=[pltpu.SMEM((devices,), jnp.int32)]
        + [pltpu.SMEM((groups * n_z * slots + 1,), jnp.int32)] * 2,
        compiler_params=params(),
        name="index",
    )(*[v[0] for v in shared])

    def contribute(ks, marks):
        own = [spans[k] for k in ks]
        direct = ks == [turned]
        outer = n_z if direct else groups
        per = groups * n_z * slots // outer
        outs, scratch = [], []
        for _, chunk in own:
            outs += arrays(outer, per * chunk + (0 if marks is None else LABEL_ROWS), channels)
            scratch.append(VMEM(((groups * n_z * slots + 1) * chunk, channels), jnp.bfloat16))
        scratch.append(pltpu.SemaphoreType.DMA((2 * len(outs),)))
        in_specs = [smem()] + [vmem()] * n_c
        args = [index] + [v[1] for v in shared]
        if marks is not None:
            in_specs.append(vmem())
            args.append(marks)
        if not direct:
            in_specs += [anywhere()] * n_c
            args += [v[2] for v in shared]
            scratch += [
                VMEM((n_c * images * top, sum(chunk for _, chunk in own), size), jnp.bfloat16),
                pltpu.SemaphoreType.DMA((n_c * len(own),)),
            ]
        base = n_c * images * top if direct else 0
        made = pl.pallas_call(
            functools.partial(
                contribute_kernel, n_c, outer, per, images, top, own, base, direct, marks is not None
            ),
            out_shape=tuple(outs),
            in_specs=in_specs,
            out_specs=(anywhere(),) * len(outs),
            scratch_shapes=scratch,
            compiler_params=params(),
        )(*args)
        return [made[i * outer : (i + 1) * outer] for i in range(len(ks))]

    def over_plane(values):
        return [
            moved_by(value, dy=g // n_x, dx=g % n_x) if g else value
            for g, value in enumerate(values)
        ]

    def over_depth(values):
        return [moved_by(value, dz=dz) if dz else value for dz, value in enumerate(values)]

    def merge(k, received, plan):
        first = plan is None
        outer = len(received)
        inner = groups * n_z // outer
        chunk = spans[k][1]
        outs = arrays(inner, blocks * chunk, channels)
        out_specs = [vmem()] * inner
        scratch = [VMEM((inner * blocks * chunk, channels), jnp.float32)]
        in_specs = [vmem()] * outer
        args = tuple(received)
        if first:
            outs.append(jax.ShapeDtypeStruct(((inner * slots + 1) * outer,), jnp.int32))
            out_specs.append(smem())
            scratch += [
                VMEM((outer, channels), jnp.int32),
                pltpu.SMEM((outer, channels), jnp.int32),
                pltpu.SemaphoreType.DMA,
            ]
        else:
            in_specs.append(smem())
            args += (plan,)
        merged = pl.pallas_call(
            functools.partial(merge_kernel, inner, outer, slots, chunk, blocks, first),
            out_shape=tuple(outs),
            in_specs=in_specs,
            out_specs=tuple(out_specs),
            scratch_shapes=scratch,
            compiler_params=params(),
        )(*args)
        return merged[:inner], merged[-1]

    (made,) = contribute([turned], labels_turned)
    received = over_depth(made)
    messages = contribute([0], labels)
    messages += contribute(list(range(1, turned)), None)
    plan, final = None, []
    for k in range(turned):
        merged, new_plan = merge(k, over_plane(messages[k]), plan)
        plan = new_plan if plan is None else plan
        final += over_depth(merged)
    last_merged = merged[0]
    merged, _ = merge(turned, received, None)
    final += over_plane(merged)
    bands = jax.ShapeDtypeStruct((3, 2, 9 * channels, 2 * channels), jnp.bfloat16)
    band1, band2 = pl.pallas_call(
        band_kernel,
        out_shape=(bands, bands),
        in_specs=[vmem(), vmem(), anywhere()],
        out_specs=(vmem(), vmem()),
        compiler_params=params(),
        name="bands",
    )(conv1_weight, conv2_weight, last_merged)
    cells = TX * TY
    lanes = DEPTH * channels
    halves = blocks // TX
    side = jax.ShapeDtypeStruct((2 * TX, lanes), jnp.bfloat16)
    left_cols, right_cols = pl.pallas_call(
        functools.partial(tail_kernel, n_z, blocks, halves),
        out_shape=(side, side),
        in_specs=[vmem()] * (2 * n_z) + [anywhere()],
        out_specs=(vmem(),) * 2,
        scratch_shapes=[VMEM((2, 2 * TX * DEPTH, channels), jnp.float32)],
        compiler_params=params(),
        name="tail",
    )(*final[: 2 * n_z], last_merged)

    def moved(value, axis, count, step):
        pairs = [(i, i + step) for i in range(count) if 0 <= i + step < count]
        return lax.ppermute(value, axis, pairs)

    left = moved(right_cols, "rows", n_rows, 1)
    right = moved(left_cols, "rows", n_rows, -1)
    wide = 80
    packed = jax.ShapeDtypeStruct((2, wide, lanes), jnp.bfloat16)
    main, first_rows, last_rows = pl.pallas_call(
        functools.partial(finish_kernel, spans, [n_z] * turned + [groups], blocks, size),
        out_shape=(jax.ShapeDtypeStruct((cells, lanes), jnp.bfloat16), packed, packed),
        in_specs=[vmem()] * (len(final) + 2) + [anywhere()],
        out_specs=(vmem(),) * 3,
        scratch_shapes=[VMEM((cells * DEPTH, channels), jnp.float32)],
        compiler_params=params(),
        name="finish",
    )(*final, left, right, band1)
    low = moved(last_rows, "frames", n_frames, 1)
    high = moved(first_rows, "frames", n_frames, -1)
    main = main.reshape(TX, TY, lanes)
    bias = (conv1_bias[None], conv2_bias[None])

    def conv_scratch(height, hidden, out):
        return (
            [VMEM((height, wide, lanes), jnp.bfloat16)] * 3
            + [VMEM((hidden, wide, lanes), jnp.bfloat16)]
            + [VMEM((hidden, TY, lanes), jnp.bfloat16)] * 2
            + [VMEM((out * TY * DEPTH, channels), jnp.float32)]
        )

    inner, kept = pl.pallas_call(
        interior_kernel,
        out_shape=(
            jax.ShapeDtypeStruct(((TX - 4) * TY * DEPTH, channels), jnp.bfloat16),
            jax.ShapeDtypeStruct((4, wide, lanes), jnp.bfloat16),
        ),
        in_specs=[vmem()] * 7,
        out_specs=(vmem(),) * 2,
        scratch_shapes=conv_scratch(TX, TX - 2, TX - 4),
        compiler_params=params(),
        name="interior",
    )(main, left, right, band1, band2, *bias)
    out = pl.pallas_call(
        border_kernel,
        out_shape=jax.ShapeDtypeStruct((cells * DEPTH, channels), jnp.bfloat16),
        in_specs=[vmem()] * 11,
        out_specs=vmem(),
        scratch_shapes=conv_scratch(8, 8, 4),
        compiler_params=params(),
        name="border",
    )(main, low, high, left, right, band1, band2, *bias, inner, kept)
    return out.reshape(TX, TY, DEPTH, channels)


def solution(mesh):
    placed = (
        P("frames", "rows", None, None),
        P("frames", "rows", None, None, None),
        P("frames", "rows", None),
        P("frames", "rows", None),
        P(),
        P(),
        P(),
        P(),
    )
    return jax.shard_map(
        shards,
        mesh=mesh,
        in_specs=placed,
        out_specs=P("frames", "rows", None, None),
        check_vma=False,
    )
```

```python
import functools

import jax
import jax.numpy as jnp
from jax import lax
from jax.experimental import pallas as pl
from jax.experimental.pallas import tpu as pltpu
from jax.sharding import PartitionSpec as P


DEPTH = 4
TX = 8
TY = 64
CORES = 2
ORDER = (0, 3, 1, 2)
LABEL_ROWS = 16
VMEM = pltpu.VMEM
LIMIT = 12 * 1024 * 1024


def vmem():
    return pl.BlockSpec(memory_space=pltpu.VMEM)


def smem():
    return pl.BlockSpec(memory_space=pltpu.SMEM)


def anywhere():
    return pl.BlockSpec(memory_space=pl.ANY)


def params():
    return pltpu.CompilerParams(vmem_limit_bytes=LIMIT)


def arrays(count, rows, channels, dtype=jnp.bfloat16):
    return [jax.ShapeDtypeStruct((rows, channels), dtype)] * count


def split_low(value, count):
    if count & (count - 1) == 0:
        return value >> (count.bit_length() - 1), value & (count - 1)
    return value // count, value % count


def apart(target, source, count):
    if count & (count - 1) == 0:
        return target ^ source
    return (target - source + count) % count


def step_to(source, step, count):
    if count & (count - 1) == 0:
        return source ^ step
    return (source + step) % count


def index_kernel(shape, slots, blocks, *refs):
    n_z, n_y, n_x, n_c = shape
    codes = refs[:n_c]
    index_ref, label_ref, label2_ref, counts, labels = refs[n_c:]
    tiles = n_z * n_y * n_x * n_c
    groups = n_y * n_x
    spare = groups * n_z * slots

    def clear(t, carry):
        counts[t] = 0
        return carry

    lax.fori_loop(0, tiles, clear, 0, unroll=16)

    def blank(s, carry):
        labels[s] = -1
        return carry

    lax.fori_loop(0, spare, blank, 0, unroll=32)
    z, y = split_low(lax.axis_index("frames"), n_y)
    x, c = split_low(lax.axis_index("rows"), n_c)
    pairs = codes[0].shape[0]
    for source in range(n_c):
        ref = codes[source]

        def place(p, carry):
            tile, block = split_low(ref[p], blocks)
            rank = counts[tile]
            counts[tile] = rank + 1
            rest, c_to = split_low(tile, n_c)
            rest, x_to = split_low(rest, n_x)
            z_to, y_to = split_low(rest, n_y)
            group = apart(y_to, y, n_y) * n_x + apart(x_to, x, n_x)
            step = apart(z_to, z, n_z)
            slot = jnp.where(c_to == c, (group * n_z + step) * slots + rank, spare)
            slot2 = jnp.where(c_to == c, (step * groups + group) * slots + rank, spare)
            index_ref[source * pairs + p] = slot
            index_ref[(n_c + source) * pairs + p] = slot2
            labels[slot] = block
            return carry

        lax.fori_loop(0, pairs, place, 0, unroll=16)
    lane = lax.broadcasted_iota(jnp.int32, (LABEL_ROWS, label_ref.shape[1]), 1)
    for g in range(groups):
        row = jnp.full(lane.shape, -1, jnp.int32)
        for k in range(n_z * slots):
            row = jnp.where(lane == k, labels[g * n_z * slots + k], row)
        label_ref[g * LABEL_ROWS : (g + 1) * LABEL_ROWS, :] = row.astype(jnp.float32).astype(jnp.bfloat16)
    for step in range(n_z):
        row = jnp.full(lane.shape, -1, jnp.int32)
        for g in range(groups):
            for rank in range(slots):
                label = labels[(g * n_z + step) * slots + rank]
                row = jnp.where(lane == g * slots + rank, label, row)
        label2_ref[step * LABEL_ROWS : (step + 1) * LABEL_ROWS, :] = row.astype(jnp.float32).astype(jnp.bfloat16)


def contribute_kernel(n_c, outer, per_group, images, top, spans, base, direct, labelled, *refs):
    index_ref = refs[0]
    features = refs[1 : 1 + n_c]
    sources = refs[1 + n_c : 1 + 2 * n_c]
    refs = refs[1 + 2 * n_c :]
    rows = sum(span[1] for span in spans)
    pairs = images * top
    size = features[0].shape[1]
    if labelled:
        label_ref, refs = refs[0], refs[1:]
    outs = refs[: outer * len(spans)]
    refs = refs[outer * len(spans) :]
    buffers, refs = refs[: len(spans)], refs[len(spans) :]
    store_sems = refs[0]
    if not direct:
        held, load_sems = refs[1:]
        loads = []
        for s in range(n_c):
            at = 0
            for i, (start, chunk) in enumerate(spans):
                loads.append(
                    pltpu.make_async_copy(
                        sources[s].at[:, pl.ds(start, chunk), :],
                        held.at[pl.ds(s * pairs, pairs), pl.ds(at, chunk)],
                        load_sems.at[s * len(spans) + i],
                    )
                )
                at += chunk
        for load in loads:
            load.start()
    for s in range(n_c):
        if not direct:
            for load in loads[s * len(spans) : (s + 1) * len(spans)]:
                load.wait()

        def image(b, carry):
            p0 = s * pairs + b * top
            if direct:
                weights = sources[s][pl.ds(pl.multiple_of(b * top * rows, top * rows), top * rows), :]
            else:
                weights = held[pl.ds(p0, top)].reshape(top * rows, size)
            product = jnp.dot(weights, features[s][b], preferred_element_type=jnp.float32)
            product = product.astype(jnp.bfloat16)
            for t in range(top):
                slot = index_ref[base + p0 + t]
                at = t * rows
                for (_, chunk), buffer in zip(spans, buffers):
                    buffer[pl.ds(pl.multiple_of(slot * chunk, chunk), chunk), :] = product[at : at + chunk]
                    at += chunk
            return carry

        lax.fori_loop(0, images, image, 0, unroll=4)
    copies = []
    for i, ((_, chunk), buffer) in enumerate(zip(spans, buffers)):
        length = per_group * chunk
        for g in range(outer):
            n = i * outer + g
            data = outs[n].at[pl.ds(0, length)] if labelled else outs[n]
            copies.append(pltpu.make_async_copy(buffer.at[pl.ds(g * length, length)], data, store_sems.at[n]))
            if labelled:
                copies.append(
                    pltpu.make_async_copy(
                        label_ref.at[pl.ds(g * LABEL_ROWS, LABEL_ROWS)],
                        outs[n].at[pl.ds(length, LABEL_ROWS)],
                        store_sems.at[outer * len(spans) + n],
                    )
                )
    for copy in copies:
        copy.start()
    for copy in copies:
        copy.wait()


def merge_kernel(n_z, groups, slots, chunk, blocks, first, *refs):
    messages = refs[:groups]
    refs = refs[groups:]
    per_group = n_z * slots
    stride = per_group + 1
    if first:
        outs = refs[:n_z]
        plan_ref, total, marks, marks_smem, sem = refs[n_z:]
        for g in range(groups):
            row = messages[g][per_group * chunk :, :].astype(jnp.float32)
            marks[g : g + 1, :] = row[0:1, :].astype(jnp.int32)
        copy = pltpu.make_async_copy(marks, marks_smem, sem)
        copy.start()
    else:
        plan_ref = refs[0]
        outs = refs[1 : 1 + n_z]
        (total,) = refs[1 + n_z :]
    total[...] = jnp.zeros_like(total)
    if first:
        copy.wait()
        for g in range(groups):

            def note(s, count):
                label = marks_smem[g, s]
                plan_ref[g * stride + 1 + count] = s * blocks + jnp.maximum(label, 0)
                return count + (label >= 0).astype(jnp.int32)

            plan_ref[g * stride] = lax.fori_loop(0, per_group, note, 0, unroll=32)
    for g in range(groups):

        def add(n, carry):
            slot, label = split_low(plan_ref[g * stride + 1 + n], blocks)
            step = split_low(slot, slots)[0]
            source = pl.ds(pl.multiple_of(slot * chunk, chunk), chunk)
            target = pl.ds(pl.multiple_of((step * blocks + label) * chunk, chunk), chunk)
            total[target, :] += messages[g][source, :].astype(jnp.float32)
            return carry

        lax.fori_loop(0, plan_ref[g * stride], add, 0)
    rows = blocks * chunk
    for step, out in enumerate(outs):
        out[...] = total[step * rows : (step + 1) * rows, :].astype(jnp.bfloat16)


def sum_parts(parts, block, chunk):
    value = None
    for ref in parts:
        part = ref[block * chunk : (block + 1) * chunk, :].astype(jnp.float32)
        value = part if value is None else value + part
    return value


def tail_kernel(n_z, blocks, halves, *refs):
    parts = refs[: 2 * n_z]
    left_ref, right_ref, columns = refs[2 * n_z + 1 :]
    chunk = parts[0].shape[0] // blocks
    width = 2 * DEPTH
    channels = columns.shape[2]
    for x in range(blocks // halves):
        value = sum_parts(parts[:n_z], x * halves, chunk)
        columns[0, x * width : (x + 1) * width, :] = value[:width]
        value = sum_parts(parts[n_z:], x * halves + halves - 1, chunk)
        columns[1, x * width : (x + 1) * width, :] = value[chunk - width :]
    cells = columns.shape[1] // DEPTH
    for side, ref in enumerate((left_ref, right_ref)):
        for z in range(DEPTH):
            part = columns[side, pl.ds(z, cells, stride=DEPTH), :].astype(jnp.bfloat16)
            ref[:, z * channels : (z + 1) * channels] = part


def finish_kernel(spans, counts, blocks, size, *refs):
    left_ref, right_ref, _, out_ref, first_ref, last_ref, total = refs[sum(counts) :]
    parts = 0
    for (start, chunk), count in zip(spans, counts):
        for block in range(blocks):
            at = block * size + start
            total[at : at + chunk, :] = sum_parts(refs[parts : parts + count], block, chunk)
        parts += count
    cells = total.shape[0] // DEPTH
    channels = total.shape[1]
    for z in range(DEPTH):
        part = total[pl.ds(z, cells, stride=DEPTH), :].astype(jnp.bfloat16)
        lanes = slice(z * channels, (z + 1) * channels)
        out_ref[:, lanes] = part
        for x in range(2):
            first_ref[x, 0:TY, lanes] = part[x * TY : (x + 1) * TY]
            last_ref[x, 0:TY, lanes] = part[cells - (2 - x) * TY : cells - (1 - x) * TY]
    rows = cells // TY
    for x in range(2):
        for ref, at in ((first_ref, x), (last_ref, rows - 2 + x)):
            ref[x, TY : TY + 2, :] = left_ref[2 * at : 2 * at + 2, :]
            ref[x, TY + 2 : TY + 4, :] = right_ref[2 * at : 2 * at + 2, :]


def band_kernel(first_ref, second_ref, after_ref, out1_ref, out2_ref):
    channels = first_ref.shape[-1]
    zero = jnp.zeros((channels, channels), jnp.bfloat16)
    for source, target in ((first_ref, out1_ref), (second_ref, out2_ref)):
        for dx in range(3):
            for half in range(2):
                for dy in range(3):
                    for k in range(3):
                        z_in = k + half
                        for j in range(2):
                            dz = z_in - (2 * half + j) + 1
                            value = source[dx, dy, dz] if 0 <= dz < 3 else zero
                            row = (dy * 3 + k) * channels
                            target[dx, half, row : row + channels, j * channels : (j + 1) * channels] = value


def silu(v):
    return v / (1.0 + jnp.exp(-v))


def convolve_half(copies, bands, half, slabs, out_rows, channels):
    total = None
    for dx in range(3):
        pieces = []
        for dy in range(3):
            lanes = slice(half * channels, (half + 3) * channels)
            height = copies[dy].shape[0] // slabs
            parts = [copies[dy][s * height + dx : s * height + dx + out_rows, :, lanes] for s in range(slabs)]
            piece = parts[0] if slabs == 1 else jnp.concatenate(parts, axis=0)
            pieces.append(piece.reshape(-1, 3 * channels))
        product = jnp.dot(
            jnp.concatenate(pieces, axis=1), bands[dx, half], preferred_element_type=jnp.float32
        )
        total = product if total is None else total + product
    return total


def volume_ends():
    ends = []
    for axis in ("frames", "rows"):
        at = lax.axis_index(axis)
        ends += [(at == 0).astype(jnp.int32), (at == lax.axis_size(axis) - 1).astype(jnp.int32)]
    return ends


def first_layer(copies, band_ref, bias_ref, slabs, out_rows, cols, put):
    ends = volume_ends()
    channels = bias_ref.shape[1]
    bias = jnp.concatenate([bias_ref[...], bias_ref[...]], axis=1)
    for half in range(2):
        total = convolve_half(copies, band_ref, half, slabs, out_rows, channels)
        value = silu(total + bias).reshape(slabs * out_rows, -1, 2 * channels)
        y_at = lax.broadcasted_iota(jnp.int32, value.shape, 1)
        keep = (y_at >= ends[2]) & (y_at < cols + 2 - ends[3])
        if slabs > 1:
            x_at = lax.broadcasted_iota(jnp.int32, value.shape, 0)
            keep = keep & (x_at >= ends[0]) & (x_at < slabs * out_rows - ends[1])
        value = jnp.where(keep, value, 0.0).astype(jnp.bfloat16)
        put(half, value)


def second_layer(copies, band_ref, bias_ref, slabs, out_rows, stage):
    channels = bias_ref.shape[1]
    cells = stage.shape[0] // DEPTH
    for half in range(2):
        total = convolve_half(copies, band_ref, half, slabs, out_rows, channels)
        for j in range(2):
            value = silu(total[:, j * channels : (j + 1) * channels] + bias_ref[...])
            stage[pl.ds(2 * half + j, cells, stride=DEPTH), :] = value


def fill(copies, x0, value, left, right):
    cols = value.shape[1]
    part = slice(x0, x0 + value.shape[0])
    copies[0][part, 2 : 2 + cols, :] = value
    copies[1][part, 1 : 1 + cols, :] = value
    copies[2][part, 0:cols, :] = value
    for i in range(value.shape[0]):
        x, j = x0 + i, 2 * i
        copies[0][x, 0:2, :] = left[j : j + 2]
        copies[1][x, 0:1, :] = left[j + 1 : j + 2]
        copies[1][x, 1 + cols : 2 + cols, :] = right[j : j + 1]
        copies[2][x, cols : 2 + cols, :] = right[j : j + 2]


def interior_kernel(
    main_ref, left_ref, right_ref, band1_ref, band2_ref, bias1_ref, bias2_ref, out_ref, kept_ref,
    copies0, copies1, copies2, hidden, shift1, shift2, stage,
):
    rows, cols = main_ref.shape[0], main_ref.shape[1]
    channels = bias1_ref.shape[1]
    copies = (copies0, copies1, copies2)
    fill(copies, 0, main_ref[...], left_ref[...], right_ref[...])
    inner = rows - 2

    def put(half, value):
        lanes = slice(half * 2 * channels, (half + 1) * 2 * channels)
        hidden[:, :, lanes] = value
        kept_ref[0:2, :, lanes] = value[0:2]
        kept_ref[2:4, :, lanes] = value[inner - 2 :]

    first_layer(copies, band1_ref, bias1_ref, 1, inner, cols, put)
    shift1[...] = hidden[:, 1 : 1 + cols, :]
    shift2[...] = hidden[:, 2 : 2 + cols, :]
    second_layer((hidden.at[:, 0:cols, :], shift1, shift2), band2_ref, bias2_ref, 1, rows - 4, stage)
    out_ref[...] = stage[...].astype(jnp.bfloat16)


def border_kernel(
    main_ref, low_ref, high_ref, left_ref, right_ref,
    band1_ref, band2_ref, bias1_ref, bias2_ref, inner_ref, kept_ref, out_ref,
    copies0, copies1, copies2, hidden, shift1, shift2, stage,
):
    channels = bias1_ref.shape[1]
    rows, cols = main_ref.shape[0], main_ref.shape[1]
    copies = (copies0, copies1, copies2)
    left, right = left_ref[...], right_ref[...]
    for x0, ref in ((0, low_ref), (6, high_ref)):
        for x in range(2):
            corner = ref[x, cols : cols + 4, :]
            fill(copies, x0 + x, ref[x : x + 1, 0:cols, :], corner[0:2], corner[2:4])
    fill(copies, 2, main_ref[0:2], left[0:4], right[0:4])
    fill(copies, 4, main_ref[rows - 2 :], left[2 * rows - 4 :], right[2 * rows - 4 :])

    def put(half, value):
        lanes = slice(half * 2 * channels, (half + 1) * 2 * channels)
        hidden[0:2, :, lanes] = value[0:2]
        hidden[6:8, :, lanes] = value[2:4]

    first_layer(copies, band1_ref, bias1_ref, 2, 2, cols, put)
    hidden[2:6, :, :] = kept_ref[...]
    shift1[...] = hidden[:, 1 : 1 + cols, :]
    shift2[...] = hidden[:, 2 : 2 + cols, :]
    second_layer((hidden.at[:, 0:cols, :], shift1, shift2), band2_ref, bias2_ref, 2, 2, stage)
    value = stage[...].astype(jnp.bfloat16)
    border = value.shape[0] // 2
    out_ref[:border, :] = value[:border]
    out_ref[border : border + inner_ref.shape[0], :] = inner_ref[...]
    out_ref[border + inner_ref.shape[0] :, :] = value[border:]


def shards(features, pair_weight, target_tile, target_block, conv1_weight, conv1_bias, conv2_weight, conv2_bias):
    images, size, channels = features.shape[1:]
    top = target_tile.shape[2]
    n_frames = lax.axis_size("frames")
    n_rows = lax.axis_size("rows")
    devices = n_frames * n_rows
    capacity = max(2, 2 * images * top // devices)
    blocks = TX * TY * DEPTH // size
    n_c = CORES if n_rows % CORES == 0 else 1
    n_x = n_rows // n_c
    n_y = n_x if n_frames % n_x == 0 else 1
    n_z = n_frames // n_y
    shape = (n_z, n_y, n_x, n_c)
    groups = n_y * n_x
    slots = n_c * capacity
    quarter = size // 4
    spans = [(part * quarter, quarter) for part in ORDER]

    def moved_by(value, dz=0, dy=0, dx=0, dc=0):
        pairs = []
        for source in range(devices):
            f, r = divmod(source, n_rows)
            z, y = divmod(f, n_y)
            x, c = divmod(r, n_c)
            z, y, x = step_to(z, dz, n_z), step_to(y, dy, n_y), step_to(x, dx, n_x)
            c = step_to(c, dc, n_c)
            pairs.append((source, ((z * n_y + y) * n_x + x) * n_c + c))
        return lax.ppermute(value, ("frames", "rows"), pairs)

    code = (target_tile * blocks + target_block).reshape(-1)
    weights = pair_weight[0].reshape(images * top, size, size)
    turned = len(spans) - 1
    begin, rows = spans[turned]
    shared = [(code, weights[:, begin : begin + rows].reshape(-1, size), features[0], weights)]
    for dc in range(1, n_c):
        shared.append(tuple(moved_by(v, dc=dc) for v in shared[0]))
    index, labels, labels_turned = pl.pallas_call(
        functools.partial(index_kernel, shape, slots, blocks),
        out_shape=(
            jax.ShapeDtypeStruct((2 * n_c * images * top,), jnp.int32),
            jax.ShapeDtypeStruct((groups * LABEL_ROWS, channels), jnp.bfloat16),
            jax.ShapeDtypeStruct((n_z * LABEL_ROWS, channels), jnp.bfloat16),
        ),
        in_specs=[smem()] * n_c,
        out_specs=(smem(), vmem(), vmem()),
        scratch_shapes=[
            pltpu.SMEM((devices,), jnp.int32),
            pltpu.SMEM((groups * n_z * slots + 1,), jnp.int32),
        ],
        compiler_params=params(),
        name="index",
    )(*[v[0] for v in shared])

    def contribute(ks, marks):
        own = [spans[k] for k in ks]
        direct = ks == [turned]
        outer = n_z if direct else groups
        per = groups * n_z * slots // outer
        outs, scratch = [], []
        for _, chunk in own:
            outs += arrays(outer, per * chunk + (0 if marks is None else LABEL_ROWS), channels)
            scratch.append(VMEM(((groups * n_z * slots + 1) * chunk, channels), jnp.bfloat16))
        scratch.append(pltpu.SemaphoreType.DMA((2 * len(outs),)))
        in_specs = [smem()] + [vmem()] * n_c + [vmem() if direct else anywhere()] * n_c
        args = [index] + [v[2] for v in shared] + [v[1 if direct else 3] for v in shared]
        if marks is not None:
            in_specs.append(vmem())
            args.append(marks)
        if not direct:
            scratch += [
                VMEM((n_c * images * top, sum(chunk for _, chunk in own), size), jnp.bfloat16),
                pltpu.SemaphoreType.DMA((n_c * len(own),)),
            ]
        base = n_c * images * top if direct else 0
        made = pl.pallas_call(
            functools.partial(
                contribute_kernel, n_c, outer, per, images, top, own, base, direct, marks is not None
            ),
            out_shape=tuple(outs),
            in_specs=in_specs,
            out_specs=(anywhere(),) * len(outs),
            scratch_shapes=scratch,
            compiler_params=params(),
        )(*args)
        return [made[i * outer : (i + 1) * outer] for i in range(len(ks))]

    def over_plane(values):
        return [
            moved_by(value, dy=g // n_x, dx=g % n_x) if g else value
            for g, value in enumerate(values)
        ]

    def over_depth(values):
        return [moved_by(value, dz=dz) if dz else value for dz, value in enumerate(values)]

    def merge(k, received, plan):
        first = plan is None
        outer = len(received)
        inner = groups * n_z // outer
        chunk = spans[k][1]
        outs = arrays(inner, blocks * chunk, channels)
        out_specs = [vmem()] * inner
        scratch = [VMEM((inner * blocks * chunk, channels), jnp.float32)]
        in_specs = [vmem()] * outer
        args = tuple(received)
        if first:
            outs.append(jax.ShapeDtypeStruct(((inner * slots + 1) * outer,), jnp.int32))
            out_specs.append(smem())
            scratch += [
                VMEM((outer, channels), jnp.int32),
                pltpu.SMEM((outer, channels), jnp.int32),
                pltpu.SemaphoreType.DMA,
            ]
        else:
            in_specs.append(smem())
            args += (plan,)
        merged = pl.pallas_call(
            functools.partial(merge_kernel, inner, outer, slots, chunk, blocks, first),
            out_shape=tuple(outs),
            in_specs=in_specs,
            out_specs=tuple(out_specs),
            scratch_shapes=scratch,
            compiler_params=params(),
        )(*args)
        return merged[:inner], merged[-1]

    (made,) = contribute([turned], labels_turned)
    received = over_depth(made)
    messages = contribute([0], labels)
    messages += contribute(list(range(1, turned)), None)
    plan, final = None, []
    for k in range(turned):
        merged, new_plan = merge(k, over_plane(messages[k]), plan)
        plan = new_plan if plan is None else plan
        final += over_depth(merged)
    last_merged = merged[0]
    merged, _ = merge(turned, received, None)
    final += over_plane(merged)
    bands = jax.ShapeDtypeStruct((3, 2, 9 * channels, 2 * channels), jnp.bfloat16)
    band1, band2 = pl.pallas_call(
        band_kernel,
        out_shape=(bands, bands),
        in_specs=[vmem(), vmem(), anywhere()],
        out_specs=(vmem(), vmem()),
        compiler_params=params(),
        name="bands",
    )(conv1_weight, conv2_weight, last_merged)
    cells = TX * TY
    lanes = DEPTH * channels
    halves = blocks // TX
    side = jax.ShapeDtypeStruct((2 * TX, lanes), jnp.bfloat16)
    left_cols, right_cols = pl.pallas_call(
        functools.partial(tail_kernel, n_z, blocks, halves),
        out_shape=(side, side),
        in_specs=[vmem()] * (2 * n_z) + [anywhere()],
        out_specs=(vmem(),) * 2,
        scratch_shapes=[VMEM((2, 2 * TX * DEPTH, channels), jnp.float32)],
        compiler_params=params(),
        name="tail",
    )(*final[: 2 * n_z], last_merged)

    def moved(value, axis, count, step):
        pairs = [(i, i + step) for i in range(count) if 0 <= i + step < count]
        return lax.ppermute(value, axis, pairs)

    left = moved(right_cols, "rows", n_rows, 1)
    right = moved(left_cols, "rows", n_rows, -1)
    packed = jax.ShapeDtypeStruct((2, TY + 8, lanes), jnp.bfloat16)
    main, first_rows, last_rows = pl.pallas_call(
        functools.partial(finish_kernel, spans, [n_z] * turned + [groups], blocks, size),
        out_shape=(jax.ShapeDtypeStruct((cells, lanes), jnp.bfloat16), packed, packed),
        in_specs=[vmem()] * (len(final) + 2) + [anywhere()],
        out_specs=(vmem(),) * 3,
        scratch_shapes=[VMEM((cells * DEPTH, channels), jnp.float32)],
        compiler_params=params(),
        name="finish",
    )(*final, left, right, band1)
    low = moved(last_rows, "frames", n_frames, 1)
    high = moved(first_rows, "frames", n_frames, -1)
    main = main.reshape(TX, TY, lanes)
    wide = 80
    bias = (conv1_bias[None], conv2_bias[None])

    def conv_scratch(height, hidden, out):
        return (
            [VMEM((height, wide, lanes), jnp.bfloat16)] * 3
            + [VMEM((hidden, wide, lanes), jnp.bfloat16)]
            + [VMEM((hidden, TY, lanes), jnp.bfloat16)] * 2
            + [VMEM((out * TY * DEPTH, channels), jnp.float32)]
        )

    inner, kept = pl.pallas_call(
        interior_kernel,
        out_shape=(
            jax.ShapeDtypeStruct(((TX - 4) * TY * DEPTH, channels), jnp.bfloat16),
            jax.ShapeDtypeStruct((4, wide, lanes), jnp.bfloat16),
        ),
        in_specs=[vmem()] * 7,
        out_specs=(vmem(),) * 2,
        scratch_shapes=conv_scratch(TX, TX - 2, TX - 4),
        compiler_params=params(),
        name="interior",
    )(main, left, right, band1, band2, *bias)
    out = pl.pallas_call(
        border_kernel,
        out_shape=jax.ShapeDtypeStruct((cells * DEPTH, channels), jnp.bfloat16),
        in_specs=[vmem()] * 11,
        out_specs=vmem(),
        scratch_shapes=conv_scratch(8, 8, 4),
        compiler_params=params(),
        name="border",
    )(main, low, high, left, right, band1, band2, *bias, inner, kept)
    return out.reshape(TX, TY, DEPTH, channels)


def solution(mesh):
    placed = (
        P("frames", "rows", None, None),
        P("frames", "rows", None, None, None),
        P("frames", "rows", None),
        P("frames", "rows", None),
        P(),
        P(),
        P(),
        P(),
    )
    return jax.shard_map(
        shards,
        mesh=mesh,
        in_specs=placed,
        out_specs=P("frames", "rows", None, None),
        check_vma=False,
    )
```
